32 devices in a mesh: gx: 8 (over z, core), gy: 4 (over y, x).
Axes of the slice: x: 2, y: 2, z: 4, core: 2. Of those that a mesh axis runs over, the one named last changes fastest.
Arguments:
- water_depth: float32 [1024, 1536], P('gx', 'gy'), may hold values from 0.3 to 3
- bed_level: float32 [1024, 1536], P('gx', 'gy'), may hold values from 0 to 2
- east_flow: float32 [1024, 1536], P('gx', 'gy'), may hold values from -4 to 4
- south_flow: float32 [1024, 1536], P('gx', 'gy'), may hold values from -4 to 4
- roughness_class: int32 [1024, 1536], P('gx', 'gy'), may hold values from 0 to 7
- wet_mask: int32 [1024, 1536], P('gx', 'gy'), may hold values 0 or 1
- soil_store: float32 [8, 1536, 128], P('gx', 'gy'), may hold values from 0.05 to 0.95
- rainfall: float32 [8, 1536, 128], P('gx', 'gy'), may hold values from 0 to 0.5
- tile_column: int32 [8, 1536, 1], P('gx', 'gy'), may hold values from 0 to 3; in each aligned block of 384 rows (0 to 383, 384 to 767, ..., all dimensions but the last counted through in order) at most 192 rows name the same one
- tile_block: int32 [8, 1536], P('gx', 'gy'), may hold values from 0 to 383
Outputs:
- new_depth: float32 [1024, 1536], P('gx', 'gy')
- new_east_flow: float32 [1024, 1536], P('gx', 'gy')
- new_south_flow: float32 [1024, 1536], P('gx', 'gy')
- new_soil: float32 [8, 1536, 128], P('gx', 'gy')
The draws below stay inside these ranges and needn't reach their ends.
Inputs may be any that keep to these rules, and one draw needn't show every extreme that they name: `tile_column`: among the 384 land blocks of one device, at most 192 name the same tile column; in some device some tile column is named by exactly 192 of them. `tile_block`: several land blocks may name the same block of a tile; some blocks are named by none.
All inputs are finite; a program needn't handle non-finite values. No bound on the sum of `wet_mask` on one device may be relied on, other than what follows from the above.
Results may differ from the reference program's by a relative error of at most 0.00002.
Values sent between devices are 32-bit elements; how exact they have to be, the bound alone decides.
A program may use at most 64 MiB of HBM per device.

```python
import math
import jax
import jax.numpy as jnp
import numpy as np

TR = 128
TC = 384
SUB = 4
LAND_DEV = 384
CAP = 192
NR = 1024
NC = 1536
N_GX = 8
N_GY = 4


def with_ends(entries, own_key, low, largest):
    dims = entries.shape
    place = [jax.random.randint(jax.random.fold_in(own_key, axis), (), 0, dims[axis]) for axis in range(len(dims))]
    entries = entries.at[tuple(place)].set(low)
    longest = dims.index(max(dims))
    place[longest] = (place[longest] + 1) % dims[longest]
    return entries.at[tuple(place)].set(largest)


def level_of(stream_key, dims, cuts, least, top_value):
    level = 1.0
    for axis_at, shards_of in cuts:
        heights = jax.random.uniform(jax.random.fold_in(jax.random.fold_in(stream_key, 6), axis_at), (shards_of,), jnp.float32, least / len(cuts), top_value / len(cuts))
        level = level * jnp.repeat(jnp.exp(heights), dims[axis_at] // shards_of).reshape((-1,) + (1,) * (len(dims) - 1 - axis_at))
    return level


def shared_out(rng, own, number, rows, number_of, top, bound, skew):
    sequence = jax.random.permutation(rng, number_of)
    heavy_load, common = load_shares(number_of, rows * top, bound, skew, True), load_shares(number_of, rows * top, bound, skew, False)
    places = jnp.arange(number_of)

    def named(tallies, turn):
        used = int((tallies > 0).sum())
        fixed = max(1, used // 4)
        shifted = fixed + (places - fixed + turn * (used - fixed)) % max(1, number_of - fixed)
        return jnp.zeros((number_of,), jnp.int32).at[sequence[jnp.where(places < fixed, places, shifted)]].set(jnp.asarray(tallies, jnp.int32))

    tallies = jnp.where(number % 4 == 0, named(heavy_load, number // 4), named(common, number - number // 4 - 1))
    mixed = jax.random.permutation(jax.random.fold_in(own, 3), number_of)
    donor, sink = mixed[0:number_of // 2 * 2:2], mixed[1:number_of // 2 * 2:2]
    slack = jnp.minimum(tallies[donor] - 1, bound - tallies[sink]) // 2
    slack = jnp.where((donor == sequence[0]) | (sink == sequence[0]) | (tallies[sink] == 0), 0, jnp.maximum(slack, 0))
    shifted = jax.random.randint(jax.random.fold_in(own, 4), (number_of // 2,), 0, 1 << 20) % (slack + 1)
    tallies = tallies.at[donor].add(-shifted).at[sink].add(shifted)
    members = jnp.searchsorted(jnp.cumsum(tallies), jnp.arange(rows * top), side="right").astype(jnp.int32)
    listing = members.reshape(top, rows).T
    listing = listing[jax.random.permutation(jax.random.fold_in(own, 1), rows)]
    turn = jax.random.randint(jax.random.fold_in(own, 2), (rows, 1), 0, top)
    return jnp.take_along_axis(listing, (jnp.arange(top)[None, :] + turn) % top, axis=1)


def load_shares(count, total, limit, slope, full):
    weights = [(1 << 20) // math.isqrt(rank ** slope) + 1 for rank in range(1, count + 1)]
    largest = limit if full else min(limit, max(-(-total // count), total * weights[0] // sum(weights)))
    least = 1 if total - largest >= count - 1 else 0
    given, surplus = [largest] + [least] * (count - 1), total - largest - least * (count - 1)
    while surplus > 0:
        free = [i for i in range(1, count) if given[i] < largest] or [i for i in range(1, count) if given[i] < limit]
        pool, left = sum([weights[i] for i in free]), surplus
        for i in free:
            addition = min(limit - given[i], max(1, left * weights[i] // pool), surplus)
            given[i] = given[i] + addition
            surplus = surplus - addition
    return np.array(given)


def noise(key, shape, width, most, pieces=(), kind=jnp.bfloat16):
    loudness = level_of(key, shape, pieces, -0.22, 0.18) if pieces else 1.0
    result = jax.random.normal(key, shape, jnp.float32) * width * loudness
    return jnp.minimum(jnp.maximum(result, -most), most).astype(kind)


def setup_inputs(seed: int = 0) -> dict:
    arg_keys = jax.random.split(jax.random.key(seed), 11)
    water_depth = jnp.clip(0.3 + 2.7 * jax.random.uniform(arg_keys[0], (NR, NC), jnp.float32) ** level_of(arg_keys[0], (NR, NC), ((0, 8), (1, 4)), -0.2, 0.2), 0.3, 3.0)
    bed_level = jnp.clip(2.0 * jax.random.uniform(arg_keys[1], (NR, NC), jnp.float32) ** level_of(arg_keys[1], (NR, NC), ((0, 8), (1, 4)), -0.2, 0.2), 0.0, 2.0)
    east_flow = noise(arg_keys[2], (NR, NC), 1.0, 4.0, ((0, 8), (1, 4)), jnp.float32)
    south_flow = noise(arg_keys[3], (NR, NC), 1.0, 4.0, ((0, 8), (1, 4)), jnp.float32)
    roughness_class = with_ends(jax.random.randint(arg_keys[4], (NR, NC), 0, 8), jax.random.fold_in(arg_keys[4], 1), 0, 7).astype(jnp.int32)
    wet_mask = with_ends((jax.random.randint(arg_keys[5], (NR, NC), 0, 8) < 7).astype(jnp.int32), jax.random.fold_in(arg_keys[5], 1), 0, 1)
    soil_store = jnp.clip(0.05 + 0.9 * jax.random.uniform(arg_keys[6], (N_GX, N_GY * LAND_DEV, 128), jnp.float32) ** level_of(arg_keys[6], (N_GX, N_GY * LAND_DEV, 128), ((0, 8), (1, 4)), -0.2, 0.2), 0.05, 0.95)
    rainfall = jnp.clip(0.5 * jax.random.uniform(arg_keys[7], (N_GX, N_GY * LAND_DEV, 128), jnp.float32) ** level_of(arg_keys[7], (N_GX, N_GY * LAND_DEV, 128), ((0, 8), (1, 4)), -0.2, 0.2), 0.0, 0.5)
    tile_column_keys = jax.random.split(jax.random.fold_in(arg_keys[8], 1), N_GX * (N_GY * LAND_DEV) // LAND_DEV)
    tile_column_turns = jax.random.permutation(jax.random.fold_in(arg_keys[8], 3), N_GX * (N_GY * LAND_DEV) // LAND_DEV)
    tile_column = jax.vmap(lambda own, number: shared_out(jax.random.fold_in(arg_keys[8], 2), own, number, LAND_DEV, N_GY, 1, CAP, 2))(tile_column_keys, tile_column_turns).reshape((N_GX, N_GY * LAND_DEV, 1))
    tile_block = with_ends(jax.random.randint(arg_keys[9], (N_GX, N_GY * LAND_DEV), 0, LAND_DEV), jax.random.fold_in(arg_keys[9], 1), 0, LAND_DEV - 1).astype(jnp.int32)
    return {"water_depth": water_depth, "bed_level": bed_level, "east_flow": east_flow, "south_flow": south_flow, "roughness_class": roughness_class, "wet_mask": wet_mask, "soil_store": soil_store, "rainfall": rainfall, "tile_column": tile_column, "tile_block": tile_block}


GRAVITY = 9.81
TIME_STEP = 1.0
CELL_WIDTH = 30.0
DEPTH_FLOOR = 0.3
INFIL_RATE = 0.5
MANNING = (0.02, 0.03, 0.035, 0.045, 0.06, 0.08, 0.10, 0.15)


def roughness(roughness_class, wet_mask):
    friction = jnp.zeros(roughness_class.shape, jnp.float32)
    for class_index, coefficient in enumerate(MANNING):
        friction = jnp.where(roughness_class == class_index, coefficient * coefficient, friction)
    return jnp.where(wet_mask > 0, friction, -1.0)


def face_flow(upper_first, upper_second, base_first, base_second, fric_first, fric_second, previous):
    flow_depth = jnp.maximum(upper_first, upper_second) - jnp.maximum(base_first, base_second)
    driving = GRAVITY * TIME_STEP * jnp.maximum(flow_depth, 0.0) * (upper_second - upper_first) / CELL_WIDTH
    mean_fric = 0.5 * (jnp.maximum(fric_first, 0.0) + jnp.maximum(fric_second, 0.0))
    damping = 1.0 + GRAVITY * TIME_STEP * mean_fric * jnp.abs(previous) / jnp.maximum(flow_depth, DEPTH_FLOOR) ** (7.0 / 3.0)
    is_open = (fric_first > 0) & (fric_second > 0)
    return jnp.where(is_open, (previous - driving) / damping, 0.0)


def advance(height, eastward, southward, bottom, friction):
    surface = bottom + height
    new_east = face_flow(surface[1:-1, :-1], surface[1:-1, 1:], bottom[1:-1, :-1], bottom[1:-1, 1:],
                         friction[1:-1, :-1], friction[1:-1, 1:], eastward[1:-1, :-1])
    new_south = face_flow(surface[:-1, 1:-1], surface[1:, 1:-1], bottom[:-1, 1:-1], bottom[1:, 1:-1],
                          friction[:-1, 1:-1], friction[1:, 1:-1], southward[:-1, 1:-1])
    change = new_east[:, :-1] - new_east[:, 1:] + new_south[:-1, :] - new_south[1:, :]
    return height[1:-1, 1:-1] + (TIME_STEP / CELL_WIDTH) * change, new_east[:, 1:], new_south[1:, :]


def to_grid(blocks):
    return blocks.reshape(N_GX, N_GY, TR, TC).transpose(0, 2, 1, 3).reshape(N_GX * TR, N_GY * TC)


def to_blocks(grid):
    return grid.reshape(N_GX, TR, N_GY, TC).transpose(0, 2, 1, 3).reshape(N_GX, N_GY * LAND_DEV, 128)


def route_row(row_runoff, row_target):
    return jax.ops.segment_sum(row_runoff, row_target, num_segments=N_GY * LAND_DEV)


def pick_row(row_blocks, row_target):
    return row_blocks[row_target]


def reference(water_depth, bed_level, east_flow, south_flow, roughness_class, wet_mask, soil_store, rainfall, tile_column, tile_block):
    runoff = rainfall * soil_store * soil_store
    target = (tile_column[:, :, 0] * LAND_DEV + tile_block).astype(jnp.int32)
    inflow = jax.vmap(route_row)(runoff, target)
    friction = roughness(roughness_class, wet_mask)
    height = water_depth + to_grid(inflow)
    eastward, southward = east_flow, south_flow
    for substep in range(SUB):
        height, eastward, southward = advance(jnp.pad(height, 1), jnp.pad(eastward, 1), jnp.pad(southward, 1),
                                              jnp.pad(bed_level, 1), jnp.pad(friction, 1))
    levels = jax.vmap(pick_row)(to_blocks(height), target)
    infiltration = INFIL_RATE * (1.0 - soil_store) * (1.0 - jnp.exp(-levels))
    new_soil = soil_store + rainfall - runoff + infiltration
    return height, eastward, southward, new_soil
```

```python
import functools

import jax
import jax.numpy as jnp
from jax import lax
from jax.experimental import pallas as pl
from jax.experimental.pallas import tpu as pltpu
from jax.sharding import PartitionSpec as P

SUB = 4
GRAVITY = 9.81
TIME_STEP = 1.0
CELL_WIDTH = 30.0
DEPTH_FLOOR = 0.3
INFIL_RATE = 0.5
MANNING = (0.02, 0.03, 0.035, 0.045, 0.06, 0.08, 0.1, 0.15)
LANES = 128
EDGE = 8
MESH = pl.DeviceIdType.MESH
AROUND = ((-1, -1), (-1, 0), (-1, 1), (0, -1), (0, 1), (1, -1), (1, 0), (1, 1))
NW, N, NE, W, E, SW, S, SE = range(8)


def split(x):
    a = x.astype(jnp.bfloat16)
    b = (x - a.astype(jnp.float32)).astype(jnp.bfloat16)
    return jnp.concatenate([a, b], axis=1)


def pick(mask, x):
    x = x if x.dtype == jnp.bfloat16 else split(x)
    y = jnp.dot(mask, x, preferred_element_type=jnp.float32)
    return y[:, :LANES] + y[:, LANES:]


def flip(i, k, n):
    if n & (n - 1):
        return None
    both, bit = 0, 1
    while bit < n:
        if k & bit:
            both = both + bit * lax.rem(i // bit, 2)
        bit *= 2
    return i + k - 2 * both


def offsets(n):
    return sorted(range(1, n), key=lambda k: bin(k).count("1"))


def east_of(x):
    return pltpu.roll(x, x.shape[1] - 1, 1)


def south_of(x):
    return pltpu.roll(x, x.shape[0] - 1, 0)


def face(eta, eta_next, base, coef, q):
    depth = jnp.maximum(eta, eta_next) - base
    driving = (GRAVITY * TIME_STEP / CELL_WIDTH) * jnp.maximum(depth, 0.0) * (eta_next - eta)
    power = jnp.exp2(jnp.log2(jnp.maximum(depth, DEPTH_FLOOR)) * (-7.0 / 3.0))
    damping = 1.0 + coef * jnp.abs(q) * power
    return jnp.where(coef > 0.0, (q - driving) / damping, 0.0)


def kernel(
    nx, ny, cap,
    depth_in, bed_in, east_in, south_in, rough_in, wet_in, soil_in, rain_in, col_in, blk_in,
    h, qe, qs, newsoil,
    bed, fric, rough, wet, land_in, index,
    base_e, base_s, coef_e, coef_s,
    give, take, give_idx, take_idx, give_lev, take_lev,
    st_rows, st_cols, st_corner, st_in_rows, st_in_cols, st_in_corner,
    h_rows, h_cols, h_in_rows, h_in_cols, h_in_corner,
    place, place_t, where_to, where_to_t, span,
    in_sem, give_r, lev_r, data_s, idx_s, idx_r, st_s, st_r, hs_s, hs_r,
):
    gx, gy = lax.axis_index("gx"), lax.axis_index("gy")
    tr, tc = rough.shape
    land = land_in.shape[1]
    chunks = tc // LANES

    inner = (pl.ds(0, tr), pl.ds(0, tc))
    loads = [
        pltpu.make_async_copy(src, dst, in_sem.at[i])
        for i, src, dst in [
            (0, col_in, index.at[0]), (0, blk_in, index.at[1]),
            (1, soil_in, land_in.at[0]), (1, rain_in, land_in.at[1]),
            (2, rough_in, rough), (2, wet_in, wet), (2, bed_in, bed.at[inner]),
            (2, east_in, qe.at[inner]), (2, south_in, qs.at[inner]),
            (3, depth_in, h.at[inner]),
        ]
    ]
    for c in loads:
        c.start()

    def settle(sem, tiles):
        ref = span.at[pl.ds(0, tiles)]
        pltpu.make_async_copy(ref, ref, sem).wait()

    def there(k):
        dx, dy = AROUND[k]
        x, y = gx + dx, gy + dy
        return (x >= 0) & (x < nx) & (y >= 0) & (y < ny)

    barrier = pltpu.get_barrier_semaphore()
    for k in range(1, ny):
        pl.semaphore_signal(
            barrier, inc=1, device_id=(gx, lax.rem(gy + k, ny)), device_id_type=MESH
        )
    total = ny - 1
    for k in (NW, N, NE, SW, S, SE):
        dx, dy = AROUND[k]

        @pl.when(there(k))
        def _(dx=dx, dy=dy):
            pl.semaphore_signal(barrier, inc=1, device_id=(gx + dx, gy + dy), device_id_type=MESH)

        total = total + there(k).astype(jnp.int32)

    for k, ref in ((N, (st_in_rows, h_in_rows)), (S, (st_in_rows, h_in_rows))):
        @pl.when(jnp.logical_not(there(k)))
        def _(k=k, ref=ref):
            for r in ref:
                r[int(k == S)] = jnp.zeros(r.shape[1:], r.dtype)
    for k, ref in ((W, (st_in_cols, h_in_cols)), (E, (st_in_cols, h_in_cols))):
        @pl.when(jnp.logical_not(there(k)))
        def _(k=k, ref=ref):
            for r in ref:
                r[int(k == E)] = jnp.zeros(r.shape[1:], r.dtype)
    for n, k in enumerate((NW, NE, SW, SE)):
        @pl.when(jnp.logical_not(there(k)))
        def _(n=n):
            for r in (st_in_corner, h_in_corner):
                r[n] = jnp.zeros(r.shape[1:], r.dtype)

    def to_peer(k):
        if k == 0:
            return gy
        peer = flip(gy, k, ny)
        return lax.rem(gy + k, ny) if peer is None else peer

    def from_peer(k):
        peer = flip(gy, k, ny)
        return lax.rem(gy + ny - k, ny) if peer is None else peer

    def send(src, dst, ss, rs, peer):
        pltpu.make_async_remote_copy(
            src_ref=src, dst_ref=dst, send_sem=ss, recv_sem=rs,
            device_id=(gx, peer), device_id_type=MESH,
        ).start()

    def arrive(dst, rs):
        pltpu.make_async_copy(dst, dst, rs).wait()

    pltpu.make_async_copy(index, index, in_sem.at[0]).wait()
    column = index[0]
    groups = max(EDGE, ny)
    is_col = lax.broadcasted_iota(jnp.int32, (groups, land), 0) == column
    before = lax.broadcasted_iota(jnp.int32, (land, land), 0) < lax.broadcasted_iota(
        jnp.int32, (land, land), 1
    )
    rank = jnp.dot(
        is_col.astype(jnp.float32).astype(jnp.bfloat16),
        before.astype(jnp.float32).astype(jnp.bfloat16),
        preferred_element_type=jnp.float32,
    )
    rank = jnp.sum(jnp.where(is_col, rank, 0.0), axis=0, keepdims=True)
    slot = column.astype(jnp.float32) * cap + rank

    block = index[1].astype(jnp.float32)
    row = jnp.floor((block + 0.5) * (1.0 / chunks))
    chunk = block - row * chunks
    line = lax.broadcasted_iota(jnp.int32, (EDGE, land), 0)
    code = jnp.where(line == 0, row + 1.0, jnp.where(line == 1, chunk, 0.0))
    code = code.astype(jnp.bfloat16)
    seat = lax.broadcasted_iota(jnp.int32, (cap, land), 0).astype(jnp.float32)

    pltpu.make_async_copy(land_in, land_in, in_sem.at[1]).wait()
    runoff = split(land_in[1] * land_in[0] * land_in[0])

    def pack(k):
        hit = (seat == slot - (to_peer(k) * cap).astype(jnp.float32)).astype(jnp.float32)
        mask = hit.astype(jnp.bfloat16)
        place[k] = mask
        owner = lax.dot_general(
            code, mask, (((1,), (1,)), ((), ())), preferred_element_type=jnp.float32
        )
        give_idx[k] = owner[1:2] * tr + owner[0:1] - 1.0
        give[k] = pick(mask, runoff)

    for n, k in enumerate(offsets(ny)):
        pack(k)
        if n == 0:
            pl.semaphore_wait(barrier, total)
        send(give_idx.at[k], take_idx.at[k], idx_s, idx_r, to_peer(k))
        send(give.at[k], take.at[k], data_s, give_r.at[k - 1], to_peer(k))
    pack(0)
    take_idx[0] = give_idx[0]

    settle(in_sem.at[2], 5 * tr * tc // (EDGE * LANES))
    kind = rough[...]
    f = jnp.zeros((tr, tc), jnp.float32)
    for i, coefficient in enumerate(MANNING):
        f = jnp.where(kind == i, coefficient * coefficient, f)
    fric[inner] = jnp.where(wet[...] > 0, f, -1.0)
    lane_low = lax.broadcasted_iota(jnp.int32, (tr, LANES), 1) < LANES // 2
    low8 = lane_low[:EDGE]
    sub_low = lax.broadcasted_iota(jnp.int32, (EDGE, 1), 0) < EDGE // 2
    half_turn = lambda x: pltpu.roll(x, EDGE // 2, 0)
    first, last = pl.ds(0, LANES), pl.ds(tc - LANES, LANES)

    def ends_of(ref):
        ends = jnp.where(lane_low, ref[0:tr, 0:LANES], ref[0:tr, tc - LANES : tc]).T
        return ends[0:EDGE], ends[LANES - EDGE :]

    pairs = ((bed, fric), (qe, qs))
    for i, (a, b) in enumerate(pairs):
        st_rows[0, i] = jnp.where(sub_low, a[0:EDGE, 0:tc], half_turn(b[0:EDGE, 0:tc]))
        st_rows[1, i] = jnp.where(
            sub_low, half_turn(b[tr - EDGE : tr, 0:tc]), a[tr - EDGE : tr, 0:tc]
        )
        (aw, ae), (bw, be) = ends_of(a), ends_of(b)
        st_cols[0, i] = jnp.where(sub_low, aw, half_turn(bw))
        st_cols[1, i] = jnp.where(sub_low, half_turn(be), ae)
    for dx in range(2):
        x, y = st_rows[dx, 0, :, first], st_rows[dx, 1, :, first]
        st_corner[dx, 0] = jnp.where(low8, x, pltpu.roll(y, LANES // 2, 1))
        x, y = st_rows[dx, 0, :, last], st_rows[dx, 1, :, last]
        st_corner[dx, 1] = jnp.where(low8, pltpu.roll(y, LANES // 2, 1), x)

    def edges(piece, tiles, ss, rs):
        def start():
            for k in (NW, NE, SW, SE, W, E, N, S):
                @pl.when(there(k))
                def _(k=k):
                    dx, dy = AROUND[k]
                    src, dst = piece(k)
                    pltpu.make_async_remote_copy(
                        src_ref=src, dst_ref=dst, send_sem=ss, recv_sem=rs,
                        device_id=(gx + dx, gy + dy), device_id_type=MESH,
                    ).start()

        def wait(sem):
            up = (gx > 0).astype(jnp.int32) + (gx < nx - 1).astype(jnp.int32)
            side = (gy > 0).astype(jnp.int32) + (gy < ny - 1).astype(jnp.int32)
            for r in range(3):
                for c in range(3):
                    n = r * tiles[0] + c * tiles[1] + r * c * tiles[2]
                    if n:
                        @pl.when((up == r) & (side == c))
                        def _(n=n):
                            settle(sem, n)

        return start, lambda: wait(rs), lambda: wait(ss)

    corner_at = {NW: 3, NE: 2, SW: 1, SE: 0}

    def st_piece(k):
        dx, dy = AROUND[k]
        if dy == 0:
            return st_rows.at[int(dx > 0)], st_in_rows.at[int(dx < 0)]
        if dx == 0:
            return st_cols.at[int(dy > 0)], st_in_cols.at[int(dy < 0)]
        return st_corner.at[int(dx > 0), int(dy > 0)], st_in_corner.at[corner_at[k]]

    def h_piece(k):
        dx, dy = AROUND[k]
        if dy == 0:
            return h_rows.at[int(dx > 0)], h_in_rows.at[int(dx < 0)]
        if dx == 0:
            return h_cols.at[int(dy > 0)], h_in_cols.at[int(dy < 0)]
        side = last if dy > 0 else first
        return h_rows.at[int(dx > 0), :, side], h_in_corner.at[corner_at[k]]

    st_start, st_wait, st_done = edges(
        st_piece, (2 * chunks, 2 * (tr // LANES), 1), st_s, st_r
    )
    h_start, h_wait, h_done = edges(h_piece, (chunks, tr // LANES, 1), hs_s, hs_r)
    st_start()

    for d in range(ny):
        place_t[d] = place[d].astype(jnp.float32).T.astype(jnp.bfloat16)

    settle_idx = take_idx.at[pl.ds(1, ny - 1)]
    if ny > 1:
        arrive(settle_idx, idx_r)
    line = lax.broadcasted_iota(jnp.int32, (land, cap), 0).astype(jnp.float32)
    for d in range(ny):
        target = (line == take_idx[d]).astype(jnp.float32)
        where_to[d] = target.astype(jnp.bfloat16)
        where_to_t[d] = target.T.astype(jnp.bfloat16)

    pltpu.make_async_copy(depth_in, h.at[inner], in_sem.at[3]).wait()
    inflow = pick(where_to[0], give[0])
    for k in offsets(ny):
        arrive(take.at[k], give_r.at[k - 1])
        inflow = inflow + pick(where_to[k], take[k])
    for c in range(chunks):
        at = (pl.ds(0, tr), pl.ds(c * LANES, LANES))
        h[at] = h[at] + inflow[c * tr : (c + 1) * tr]

    h_rows[0] = h[0:EDGE, 0:tc]
    h_rows[1] = h[tr - EDGE : tr, 0:tc]
    h_cols[0], h_cols[1] = ends_of(h)
    h_start()

    def sides(west, east):
        side = jnp.concatenate(
            [east, jnp.zeros((LANES - 2 * EDGE, tr), jnp.float32), west], axis=0
        )
        return side.T

    def quarter(nw, ne, sw, se):
        return jnp.where(low8, jnp.where(sub_low, se, ne), jnp.where(sub_low, sw, nw))

    st_wait()
    corners = [st_in_corner[n] for n in range(4)]
    nw, ne, sw, se = corners
    for i, (a, b) in enumerate(pairs):
        up, down = st_in_rows[0, i], st_in_rows[1, i]
        a[tr : tr + EDGE, 0:tc] = jnp.where(sub_low, down, up)
        b[tr : tr + EDGE, 0:tc] = half_turn(jnp.where(sub_low, up, down))
        west, east = st_in_cols[0, i], st_in_cols[1, i]
        a[0:tr, tc : tc + LANES] = sides(west, east)
        b[0:tr, tc : tc + LANES] = sides(half_turn(west), half_turn(east))
        if i == 0:
            ca, cb = quarter(nw, ne, sw, se), half_turn(quarter(sw, se, nw, ne))
        else:
            ca = pltpu.roll(quarter(ne, nw, se, sw), LANES // 2, 1)
            cb = half_turn(pltpu.roll(quarter(se, sw, ne, nw), LANES // 2, 1))
        a[tr : tr + EDGE, tc : tc + LANES] = ca
        b[tr : tr + EDGE, tc : tc + LANES] = cb
    b, fr = bed[...], fric[...]
    b_e, f_e, b_s, f_s = east_of(b), east_of(fr), south_of(b), south_of(fr)
    half = 0.5 * GRAVITY * TIME_STEP
    base_e[...] = jnp.maximum(b, b_e)
    base_s[...] = jnp.maximum(b, b_s)
    coef_e[...] = jnp.where((fr > 0.0) & (f_e > 0.0), half * (fr + f_e), -1.0)
    coef_s[...] = jnp.where((fr > 0.0) & (f_s > 0.0), half * (fr + f_s), -1.0)

    h_wait()
    h[tr : tr + EDGE, 0:tc] = jnp.where(sub_low, h_in_rows[1], h_in_rows[0])
    h[0:tr, tc : tc + LANES] = sides(h_in_cols[0], h_in_cols[1])
    h[tr : tr + EDGE, tc : tc + LANES] = quarter(*[h_in_corner[n] for n in range(4)])

    for step in range(SUB):
        eta = h[...] + bed[...]
        e = face(eta, east_of(eta), base_e[...], coef_e[...], qe[...])
        s = face(eta, south_of(eta), base_s[...], coef_s[...], qs[...])
        qe[...] = e
        qs[...] = s
        h[...] = h[...] + (TIME_STEP / CELL_WIDTH) * (
            pltpu.roll(e, 1, 1) - e + pltpu.roll(s, 1, 0) - s
        )

    blocks = split(jnp.concatenate(
        [h[0:tr, c * LANES : (c + 1) * LANES] for c in range(chunks)], axis=0
    ))
    for k in offsets(ny):
        give_lev[k] = pick(where_to_t[k], blocks)
        send(give_lev.at[k], take_lev.at[k], data_s, lev_r.at[k - 1], from_peer(k))
    mine = pick(place_t[0], pick(where_to_t[0], blocks))
    for k in offsets(ny):
        arrive(take_lev.at[k], lev_r.at[k - 1])
        mine = mine + pick(place_t[k], take_lev[k])
    store, rain = land_in[0], land_in[1]
    runoff = rain * store * store
    newsoil[...] = (
        store + rain - runoff + INFIL_RATE * (1.0 - store) * (1.0 - jnp.exp(-mine))
    )
    if ny > 1:
        arrive(settle_idx, idx_s)
        settle(data_s, 2 * (ny - 1) * cap // EDGE)
    st_done()
    h_done()


def write_out(h, qe, qs, newsoil, depth_out, east_out, south_out, soil_out, sem):
    tr, tc = depth_out.shape
    inner = (pl.ds(0, tr), pl.ds(0, tc))
    copies = [
        pltpu.make_async_copy(src, dst, sem.at[i])
        for i, (src, dst) in enumerate(
            [
                (h.at[inner], depth_out), (qe.at[inner], east_out),
                (qs.at[inner], south_out), (newsoil, soil_out),
            ]
        )
    ]
    for c in copies:
        c.start()
    for c in copies:
        c.wait()


def local(depth, bed, east, south, rough, wet, soil, rain, column, block):
    nx, ny = lax.axis_size("gx"), lax.axis_size("gy")
    tr, tc = depth.shape
    land = soil.shape[1]
    cap = 2 * land // ny
    grid = (tr + EDGE, tc + LANES)
    f32, bf16, i32 = jnp.float32, jnp.bfloat16, jnp.int32
    v = pltpu.VMEM
    dma = pltpu.SemaphoreType.DMA
    peers = max(1, ny - 1)

    def edge_bufs(k):
        return [v((2, *k, EDGE, tc), f32), v((2, *k, EDGE, tr), f32)]

    corners = v((2, 2, EDGE, LANES), f32)
    in_corners = v((4, EDGE, LANES), f32)
    span = max(5 * tr * tc, 2 * peers * cap * LANES, 4 * EDGE * (2 * tc + 2 * tr + 4 * LANES))
    any_ = pl.BlockSpec(memory_space=pltpu.MemorySpace.HBM)
    vmem = pl.BlockSpec(memory_space=pltpu.VMEM)
    shape = jax.ShapeDtypeStruct
    out = pl.pallas_call(
        functools.partial(kernel, nx, ny, cap),
        out_shape=[shape(grid, f32)] * 3 + [shape((land, LANES), f32)],
        in_specs=[any_] * 10,
        out_specs=[vmem] * 4,
        scratch_shapes=[v(grid, f32)] * 2
        + [v((tr, tc), i32)] * 2
        + [v((2, land, LANES), f32), v((2, 1, land), i32)]
        + [v(grid, f32)] * 4
        + [v((ny, cap, LANES), f32)] * 2
        + [v((ny, 1, cap), f32)] * 2
        + [v((ny, cap, LANES), f32)] * 2
        + edge_bufs((2,)) + [corners] + edge_bufs((2,)) + [in_corners]
        + edge_bufs(()) + edge_bufs(()) + [in_corners]
        + [v((ny, cap, land), bf16), v((ny, land, cap), bf16)]
        + [v((ny, land, cap), bf16), v((ny, cap, land), bf16)]
        + [v((span // (EDGE * LANES), EDGE, LANES), f32)]
        + [dma((4,))]
        + [dma((peers,))] * 2
        + [dma] * 7,
        compiler_params=pltpu.CompilerParams(collective_id=0, has_side_effects=True, vmem_limit_bytes=24 << 20
        ),
    )(
        *(
            pltpu.with_memory_space_constraint(x, pltpu.MemorySpace.HBM)
            for x in (
                depth, bed, east, south, rough, wet, soil[0], rain[0],
                column.reshape(1, land), block,
            )
        )
    )
    out = pl.pallas_call(
        write_out,
        out_shape=[shape((tr, tc), f32)] * 3 + [shape((land, LANES), f32)],
        in_specs=[vmem] * 4,
        out_specs=[any_] * 4,
        scratch_shapes=[dma((4,))],
        compiler_params=pltpu.CompilerParams(vmem_limit_bytes=8 << 20),
    )(*out)
    return out[0], out[1], out[2], out[3][None]


def solution(mesh):
    grid = P("gx", "gy")
    blocks = P("gx", "gy", None)
    return jax.shard_map(
        local, mesh=mesh,
        in_specs=(grid,) * 6 + (blocks,) * 3 + (grid,),
        out_specs=(grid,) * 3 + (blocks,),
        check_vma=False,
    )
```

```python
import functools

import jax
import jax.numpy as jnp
from jax import lax
from jax.experimental import pallas as pl
from jax.experimental.pallas import tpu as pltpu
from jax.sharding import PartitionSpec as P

SUB = 4
GRAVITY = 9.81
TIME_STEP = 1.0
CELL_WIDTH = 30.0
DEPTH_FLOOR = 0.3
INFIL_RATE = 0.5
MANNING = (0.02, 0.03, 0.035, 0.045, 0.06, 0.08, 0.1, 0.15)
LANES = 128
EDGE = 8
MESH = pl.DeviceIdType.MESH
AROUND = ((-1, -1), (-1, 0), (-1, 1), (0, -1), (0, 1), (1, -1), (1, 0), (1, 1))
NW, N, NE, W, E, SW, S, SE = range(8)


def split(x):
    a = x.astype(jnp.bfloat16)
    b = (x - a.astype(jnp.float32)).astype(jnp.bfloat16)
    return jnp.concatenate([a, b], axis=1)


def pick(mask, x):
    x = x if x.dtype == jnp.bfloat16 else split(x)
    y = jnp.dot(mask, x, preferred_element_type=jnp.float32)
    return y[:, :LANES] + y[:, LANES:]


def flip(i, k, n):
    if n & (n - 1):
        return None
    both, bit = 0, 1
    while bit < n:
        if k & bit:
            both = both + bit * lax.rem(i // bit, 2)
        bit *= 2
    return i + k - 2 * both


def offsets(n):
    return sorted(range(1, n), key=lambda k: bin(k).count("1"))


def east_of(x):
    return pltpu.roll(x, x.shape[1] - 1, 1)


def south_of(x):
    return pltpu.roll(x, x.shape[0] - 1, 0)


def face(eta, eta_next, base, coef, q):
    depth = jnp.maximum(eta, eta_next) - base
    driving = (GRAVITY * TIME_STEP / CELL_WIDTH) * jnp.maximum(depth, 0.0) * (eta_next - eta)
    power = jnp.exp2(jnp.log2(jnp.maximum(depth, DEPTH_FLOOR)) * (-7.0 / 3.0))
    damping = 1.0 + coef * jnp.abs(q) * power
    return jnp.where(coef > 0.0, (q - driving) / damping, 0.0)


def kernel(
    nx, ny, cap,
    depth_in, bed_in, east_in, south_in, rough_in, wet_in, soil_in, rain_in, col_in, blk_in,
    h, qe, qs, newsoil,
    bed, fric, rough, wet, land_in, index,
    tile_face, rim, rim_face, flank, flank_face,
    give, take, give_idx, take_idx, give_lev, take_lev,
    st_rows, st_cols, st_corner, st_in_rows, st_in_cols, st_in_corner,
    h_rows, h_cols, h_in_rows, h_in_cols, h_in_corner,
    place, place_t, where_to, where_to_t, span,
    in_sem, give_r, lev_r, data_s, idx_s, idx_r, st_s, st_r, hs_s, hs_r,
):
    gx, gy = lax.axis_index("gx"), lax.axis_index("gy")
    tr, tc = rough.shape
    land = land_in.shape[1]
    chunks = tc // LANES

    loads = [
        pltpu.make_async_copy(src, dst, in_sem.at[i])
        for i, src, dst in [
            (0, col_in, index.at[0]), (0, blk_in, index.at[1]),
            (1, soil_in, land_in.at[0]), (1, rain_in, land_in.at[1]),
            (2, rough_in, rough), (2, wet_in, wet), (2, bed_in, bed),
            (2, east_in, qe), (2, south_in, qs), (3, depth_in, h),
        ]
    ]
    for c in loads:
        c.start()

    def settle(sem, tiles):
        ref = span.at[pl.ds(0, tiles)]
        pltpu.make_async_copy(ref, ref, sem).wait()

    def there(k):
        dx, dy = AROUND[k]
        x, y = gx + dx, gy + dy
        return (x >= 0) & (x < nx) & (y >= 0) & (y < ny)

    barrier = pltpu.get_barrier_semaphore()
    for k in range(1, ny):
        pl.semaphore_signal(
            barrier, inc=1, device_id=(gx, lax.rem(gy + k, ny)), device_id_type=MESH
        )
    total = ny - 1
    for k in (NW, N, NE, SW, S, SE):
        dx, dy = AROUND[k]

        @pl.when(there(k))
        def _(dx=dx, dy=dy):
            pl.semaphore_signal(barrier, inc=1, device_id=(gx + dx, gy + dy), device_id_type=MESH)

        total = total + there(k).astype(jnp.int32)

    for k, ref in ((N, (st_in_rows, h_in_rows)), (S, (st_in_rows, h_in_rows))):
        @pl.when(jnp.logical_not(there(k)))
        def _(k=k, ref=ref):
            for r in ref:
                r[int(k == S)] = jnp.zeros(r.shape[1:], r.dtype)
    for k, ref in ((W, (st_in_cols, h_in_cols)), (E, (st_in_cols, h_in_cols))):
        @pl.when(jnp.logical_not(there(k)))
        def _(k=k, ref=ref):
            for r in ref:
                r[int(k == E)] = jnp.zeros(r.shape[1:], r.dtype)
    for n, k in enumerate((NW, NE, SW, SE)):
        @pl.when(jnp.logical_not(there(k)))
        def _(n=n):
            for r in (st_in_corner, h_in_corner):
                r[n] = jnp.zeros(r.shape[1:], r.dtype)

    def to_peer(k):
        if k == 0:
            return gy
        peer = flip(gy, k, ny)
        return lax.rem(gy + k, ny) if peer is None else peer

    def from_peer(k):
        peer = flip(gy, k, ny)
        return lax.rem(gy + ny - k, ny) if peer is None else peer

    def send(src, dst, ss, rs, peer):
        pltpu.make_async_remote_copy(
            src_ref=src, dst_ref=dst, send_sem=ss, recv_sem=rs,
            device_id=(gx, peer), device_id_type=MESH,
        ).start()

    def arrive(dst, rs):
        pltpu.make_async_copy(dst, dst, rs).wait()

    pltpu.make_async_copy(index, index, in_sem.at[0]).wait()
    column = index[0]
    groups = max(EDGE, ny)
    is_col = lax.broadcasted_iota(jnp.int32, (groups, land), 0) == column
    before = lax.broadcasted_iota(jnp.int32, (land, land), 0) < lax.broadcasted_iota(
        jnp.int32, (land, land), 1
    )
    rank = jnp.dot(
        is_col.astype(jnp.float32).astype(jnp.bfloat16),
        before.astype(jnp.float32).astype(jnp.bfloat16),
        preferred_element_type=jnp.float32,
    )
    rank = jnp.sum(jnp.where(is_col, rank, 0.0), axis=0, keepdims=True)
    slot = column.astype(jnp.float32) * cap + rank

    block = index[1].astype(jnp.float32)
    row = jnp.floor((block + 0.5) * (1.0 / chunks))
    chunk = block - row * chunks
    line = lax.broadcasted_iota(jnp.int32, (EDGE, land), 0)
    code = jnp.where(line == 0, row + 1.0, jnp.where(line == 1, chunk, 0.0))
    code = code.astype(jnp.bfloat16)
    seat = lax.broadcasted_iota(jnp.int32, (cap, land), 0).astype(jnp.float32)

    pltpu.make_async_copy(land_in, land_in, in_sem.at[1]).wait()
    runoff = split(land_in[1] * land_in[0] * land_in[0])

    def pack(k):
        hit = (seat == slot - (to_peer(k) * cap).astype(jnp.float32)).astype(jnp.float32)
        mask = hit.astype(jnp.bfloat16)
        place[k] = mask
        owner = lax.dot_general(
            code, mask, (((1,), (1,)), ((), ())), preferred_element_type=jnp.float32
        )
        give_idx[k] = owner[1:2] * tr + owner[0:1] - 1.0
        give[k] = pick(mask, runoff)

    for n, k in enumerate(offsets(ny)):
        pack(k)
        if n == 0:
            pl.semaphore_wait(barrier, total)
        send(give_idx.at[k], take_idx.at[k], idx_s, idx_r, to_peer(k))
        send(give.at[k], take.at[k], data_s, give_r.at[k - 1], to_peer(k))
    pack(0)
    take_idx[0] = give_idx[0]

    settle(in_sem.at[2], 5 * tr * tc // (EDGE * LANES))
    kind = rough[...]
    f = jnp.zeros((tr, tc), jnp.float32)
    for i, coefficient in enumerate(MANNING):
        f = jnp.where(kind == i, coefficient * coefficient, f)
    fric[...] = jnp.where(wet[...] > 0, f, -1.0)
    lane_low = lax.broadcasted_iota(jnp.int32, (tr, LANES), 1) < LANES // 2
    low8 = lane_low[:EDGE]
    sub_low = lax.broadcasted_iota(jnp.int32, (EDGE, 1), 0) < EDGE // 2
    half_turn = lambda x: pltpu.roll(x, EDGE // 2, 0)
    first, last = pl.ds(0, LANES), pl.ds(tc - LANES, LANES)

    def ends_of(ref):
        ends = jnp.where(lane_low, ref[0:tr, 0:LANES], ref[0:tr, tc - LANES : tc]).T
        return ends[0:EDGE], ends[LANES - EDGE :]

    pairs = ((bed, fric), (qe, qs))
    for i, (a, b) in enumerate(pairs):
        st_rows[0, i] = jnp.where(sub_low, a[0:EDGE, 0:tc], half_turn(b[0:EDGE, 0:tc]))
        st_rows[1, i] = jnp.where(
            sub_low, half_turn(b[tr - EDGE : tr, 0:tc]), a[tr - EDGE : tr, 0:tc]
        )
        (aw, ae), (bw, be) = ends_of(a), ends_of(b)
        st_cols[0, i] = jnp.where(sub_low, aw, half_turn(bw))
        st_cols[1, i] = jnp.where(sub_low, half_turn(be), ae)
    for dx in range(2):
        x, y = st_rows[dx, 0, :, first], st_rows[dx, 1, :, first]
        st_corner[dx, 0] = jnp.where(low8, x, pltpu.roll(y, LANES // 2, 1))
        x, y = st_rows[dx, 0, :, last], st_rows[dx, 1, :, last]
        st_corner[dx, 1] = jnp.where(low8, pltpu.roll(y, LANES // 2, 1), x)

    def edges(piece, tiles, ss, rs):
        def start():
            for k in (NW, NE, SW, SE, W, E, N, S):
                @pl.when(there(k))
                def _(k=k):
                    dx, dy = AROUND[k]
                    src, dst = piece(k)
                    pltpu.make_async_remote_copy(
                        src_ref=src, dst_ref=dst, send_sem=ss, recv_sem=rs,
                        device_id=(gx + dx, gy + dy), device_id_type=MESH,
                    ).start()

        def wait(sem):
            up = (gx > 0).astype(jnp.int32) + (gx < nx - 1).astype(jnp.int32)
            side = (gy > 0).astype(jnp.int32) + (gy < ny - 1).astype(jnp.int32)
            for r in range(3):
                for c in range(3):
                    n = r * tiles[0] + c * tiles[1] + r * c * tiles[2]
                    if n:
                        @pl.when((up == r) & (side == c))
                        def _(n=n):
                            settle(sem, n)

        return start, lambda: wait(rs), lambda: wait(ss)

    corner_at = {NW: 3, NE: 2, SW: 1, SE: 0}

    def st_piece(k):
        dx, dy = AROUND[k]
        if dy == 0:
            return st_rows.at[int(dx > 0)], st_in_rows.at[int(dx < 0)]
        if dx == 0:
            return st_cols.at[int(dy > 0)], st_in_cols.at[int(dy < 0)]
        return st_corner.at[int(dx > 0), int(dy > 0)], st_in_corner.at[corner_at[k]]

    def h_piece(k):
        dx, dy = AROUND[k]
        if dy == 0:
            return h_rows.at[int(dx > 0)], h_in_rows.at[int(dx < 0)]
        if dx == 0:
            return h_cols.at[int(dy > 0)], h_in_cols.at[int(dy < 0)]
        side = last if dy > 0 else first
        return h_rows.at[int(dx > 0), :, side], h_in_corner.at[corner_at[k]]

    st_start, st_wait, st_done = edges(
        st_piece, (2 * chunks, 2 * (tr // LANES), 1), st_s, st_r
    )
    h_start, h_wait, h_done = edges(h_piece, (chunks, tr // LANES, 1), hs_s, hs_r)
    st_start()

    lane = lax.broadcasted_iota(jnp.int32, (tr, LANES), 1)
    own = lane < LANES // 2

    def keep(x, i):
        rim[i, 0:EDGE] = x[tr - EDGE : tr, 0:tc]
        rim[i, 2 * EDGE : 3 * EDGE] = x[0:EDGE, 0:tc]
        flank[i, 0:tr] = jnp.where(
            lane < LANES // 4,
            x[0:tr, 0:LANES],
            pltpu.roll(x[0:tr, tc - LANES : tc], LANES // 2, 1),
        )

    def faces(b, fr, out):
        b_e, f_e, b_s, f_s = east_of(b), east_of(fr), south_of(b), south_of(fr)
        half = 0.5 * GRAVITY * TIME_STEP
        out[0] = jnp.maximum(b, b_e)
        out[1] = jnp.maximum(b, b_s)
        out[2] = jnp.where((fr > 0.0) & (f_e > 0.0), half * (fr + f_e), -1.0)
        out[3] = jnp.where((fr > 0.0) & (f_s > 0.0), half * (fr + f_s), -1.0)

    def substep(depth, b, e, s, out):
        eta = depth + b
        e = face(eta, east_of(eta), out[0], out[2], e)
        s = face(eta, south_of(eta), out[1], out[3], s)
        depth = depth + (TIME_STEP / CELL_WIDTH) * (
            pltpu.roll(e, 1, 1) - e + pltpu.roll(s, 1, 0) - s
        )
        return depth, e, s

    for i, x in enumerate((bed, fric, qe, qs)):
        keep(x, i)
    faces(bed[...], fric[...], tile_face)

    for d in range(ny):
        place_t[d] = place[d].astype(jnp.float32).T.astype(jnp.bfloat16)

    settle_idx = take_idx.at[pl.ds(1, ny - 1)]
    if ny > 1:
        arrive(settle_idx, idx_r)
    line = lax.broadcasted_iota(jnp.int32, (land, cap), 0).astype(jnp.float32)
    for d in range(ny):
        target = (line == take_idx[d]).astype(jnp.float32)
        where_to[d] = target.astype(jnp.bfloat16)
        where_to_t[d] = target.T.astype(jnp.bfloat16)

    pltpu.make_async_copy(depth_in, h, in_sem.at[3]).wait()
    inflow = pick(where_to[0], give[0])
    for k in offsets(ny):
        arrive(take.at[k], give_r.at[k - 1])
        inflow = inflow + pick(where_to[k], take[k])
    for c in range(chunks):
        at = (pl.ds(0, tr), pl.ds(c * LANES, LANES))
        h[at] = h[at] + inflow[c * tr : (c + 1) * tr]

    h_rows[0] = h[0:EDGE, 0:tc]
    h_rows[1] = h[tr - EDGE : tr, 0:tc]
    h_cols[0], h_cols[1] = ends_of(h)
    h_start()
    keep(h, 4)

    for step in range(SUB):
        h[...], qe[...], qs[...] = substep(h[...], bed[...], qe[...], qs[...], tile_face)

    gap = jnp.zeros((LANES // 2 - 2 * EDGE, tr), jnp.float32)
    half_gap = jnp.zeros((LANES // 2, tr), jnp.float32)
    lane8 = lane[:EDGE]

    def wrap(i, halo, west, east, corner_w, corner_e):
        side = jnp.concatenate([half_gap, east, gap, west], axis=0)
        rim[i, EDGE : 2 * EDGE] = halo
        flank[i, 0:tr] = jnp.where(own, flank[i, 0:tr], side.T)
        corner = jnp.where(lane8 < 3 * LANES // 4, corner_e, corner_w)
        far = pltpu.roll(halo[:, tc - LANES :], LANES // 2, 1)
        line = jnp.where(lane8 < LANES // 4, halo[:, :LANES], far)
        flank[i, tr : tr + EDGE] = jnp.where(low8, line, corner)

    def turn(x):
        return pltpu.roll(x, LANES // 2, 1)

    st_wait()
    nw, ne, sw, se = [st_in_corner[n] for n in range(4)]
    west_a, west_b = jnp.where(sub_low, sw, nw), half_turn(jnp.where(sub_low, nw, sw))
    east_a, east_b = jnp.where(sub_low, se, ne), half_turn(jnp.where(sub_low, ne, se))
    for i in range(2):
        up, down = st_in_rows[0, i], st_in_rows[1, i]
        west, east = st_in_cols[0, i], st_in_cols[1, i]
        cw = (west_a, west_b) if i == 0 else (turn(west_a), turn(west_b))
        ce = (turn(east_a), turn(east_b)) if i == 0 else (east_a, east_b)
        wrap(2 * i, jnp.where(sub_low, down, up), west, east, cw[0], ce[0])
        wrap(
            2 * i + 1, half_turn(jnp.where(sub_low, up, down)), half_turn(west),
            half_turn(east), cw[1], ce[1],
        )
    faces(rim[0], rim[1], rim_face)
    faces(flank[0], flank[1], flank_face)

    h_wait()
    nw, ne, sw, se = [h_in_corner[n] for n in range(4)]
    wrap(
        4, jnp.where(sub_low, h_in_rows[1], h_in_rows[0]), h_in_cols[0], h_in_cols[1],
        jnp.where(sub_low, sw, nw), turn(jnp.where(sub_low, se, ne)),
    )

    for step in range(SUB):
        for x, out in ((rim, rim_face), (flank, flank_face)):
            x[4], x[2], x[3] = substep(x[4], x[0], x[2], x[3], out)

    reach = EDGE // 2
    for i, x in ((4, h), (2, qe), (3, qs)):
        x[0:EDGE] = jnp.where(sub_low, rim[i, 2 * EDGE : 3 * EDGE], x[0:EDGE])
        x[tr - EDGE : tr] = jnp.where(sub_low, x[tr - EDGE : tr], rim[i, 0:EDGE])
        edge = flank[i, 0:tr]
        x[:, 0:LANES] = jnp.where(lane < reach, edge, x[:, 0:LANES])
        x[:, tc - LANES : tc] = jnp.where(
            lane >= LANES - reach, turn(edge), x[:, tc - LANES : tc]
        )

    blocks = split(jnp.concatenate(
        [h[0:tr, c * LANES : (c + 1) * LANES] for c in range(chunks)], axis=0
    ))
    for k in offsets(ny):
        give_lev[k] = pick(where_to_t[k], blocks)
        send(give_lev.at[k], take_lev.at[k], data_s, lev_r.at[k - 1], from_peer(k))
    mine = pick(place_t[0], pick(where_to_t[0], blocks))
    for k in offsets(ny):
        arrive(take_lev.at[k], lev_r.at[k - 1])
        mine = mine + pick(place_t[k], take_lev[k])
    store, rain = land_in[0], land_in[1]
    runoff = rain * store * store
    newsoil[...] = (
        store + rain - runoff + INFIL_RATE * (1.0 - store) * (1.0 - jnp.exp(-mine))
    )
    if ny > 1:
        arrive(settle_idx, idx_s)
        settle(data_s, 2 * (ny - 1) * cap // EDGE)
    st_done()
    h_done()


def write_out(h, qe, qs, newsoil, depth_out, east_out, south_out, soil_out, sem):
    copies = [
        pltpu.make_async_copy(src, dst, sem.at[i])
        for i, (src, dst) in enumerate(
            [
                (h, depth_out), (qe, east_out), (qs, south_out), (newsoil, soil_out),
            ]
        )
    ]
    for c in copies:
        c.start()
    for c in copies:
        c.wait()


def local(depth, bed, east, south, rough, wet, soil, rain, column, block):
    nx, ny = lax.axis_size("gx"), lax.axis_size("gy")
    tr, tc = depth.shape
    land = soil.shape[1]
    cap = 2 * land // ny
    grid = (tr, tc)
    rim, flank = (3 * EDGE, tc), (tr + EDGE, LANES)
    f32, bf16, i32 = jnp.float32, jnp.bfloat16, jnp.int32
    v = pltpu.VMEM
    dma = pltpu.SemaphoreType.DMA
    peers = max(1, ny - 1)

    def edge_bufs(k):
        return [v((2, *k, EDGE, tc), f32), v((2, *k, EDGE, tr), f32)]

    corners = v((2, 2, EDGE, LANES), f32)
    in_corners = v((4, EDGE, LANES), f32)
    span = max(5 * tr * tc, 2 * peers * cap * LANES, 4 * EDGE * (2 * tc + 2 * tr + 4 * LANES))
    any_ = pl.BlockSpec(memory_space=pltpu.MemorySpace.HBM)
    vmem = pl.BlockSpec(memory_space=pltpu.VMEM)
    shape = jax.ShapeDtypeStruct
    out = pl.pallas_call(
        functools.partial(kernel, nx, ny, cap),
        out_shape=[shape(grid, f32)] * 3 + [shape((land, LANES), f32)],
        in_specs=[any_] * 10,
        out_specs=[vmem] * 4,
        scratch_shapes=[v(grid, f32)] * 2
        + [v((tr, tc), i32)] * 2
        + [v((2, land, LANES), f32), v((2, 1, land), i32)]
        + [v((4, *grid), f32), v((5, *rim), f32), v((4, *rim), f32)]
        + [v((5, *flank), f32), v((4, *flank), f32)]
        + [v((ny, cap, LANES), f32)] * 2
        + [v((ny, 1, cap), f32)] * 2
        + [v((ny, cap, LANES), f32)] * 2
        + edge_bufs((2,)) + [corners] + edge_bufs((2,)) + [in_corners]
        + edge_bufs(()) + edge_bufs(()) + [in_corners]
        + [v((ny, cap, land), bf16), v((ny, land, cap), bf16)]
        + [v((ny, land, cap), bf16), v((ny, cap, land), bf16)]
        + [v((span // (EDGE * LANES), EDGE, LANES), f32)]
        + [dma((4,))]
        + [dma((peers,))] * 2
        + [dma] * 7,
        compiler_params=pltpu.CompilerParams(collective_id=0, has_side_effects=True, vmem_limit_bytes=24 << 20
        ),
    )(
        *(
            pltpu.with_memory_space_constraint(x, pltpu.MemorySpace.HBM)
            for x in (
                depth, bed, east, south, rough, wet, soil[0], rain[0],
                column.reshape(1, land), block,
            )
        )
    )
    out = pl.pallas_call(
        write_out,
        out_shape=[shape((tr, tc), f32)] * 3 + [shape((land, LANES), f32)],
        in_specs=[vmem] * 4,
        out_specs=[any_] * 4,
        scratch_shapes=[dma((4,))],
        compiler_params=pltpu.CompilerParams(vmem_limit_bytes=8 << 20),
    )(*out)
    return out[0], out[1], out[2], out[3][None]


def solution(mesh):
    grid = P("gx", "gy")
    blocks = P("gx", "gy", None)
    return jax.shard_map(
        local, mesh=mesh,
        in_specs=(grid,) * 6 + (blocks,) * 3 + (grid,),
        out_specs=(grid,) * 3 + (blocks,),
        check_vma=False,
    )
```

```python
import functools

import jax
import jax.numpy as jnp
from jax import lax
from jax.experimental import pallas as pl
from jax.experimental.pallas import tpu as pltpu
from jax.sharding import PartitionSpec as P

SUB = 4
GRAVITY = 9.81
TIME_STEP = 1.0
CELL_WIDTH = 30.0
DEPTH_FLOOR = 0.3
INFIL_RATE = 0.5
MANNING = (0.02, 0.03, 0.035, 0.045, 0.06, 0.08, 0.1, 0.15)
LANES = 128
EDGE = 8
MESH = pl.DeviceIdType.MESH
AROUND = ((-1, -1), (-1, 0), (-1, 1), (0, -1), (0, 1), (1, -1), (1, 0), (1, 1))
NW, N, NE, W, E, SW, S, SE = range(8)


def split(x):
    a = x.astype(jnp.bfloat16)
    b = (x - a.astype(jnp.float32)).astype(jnp.bfloat16)
    return jnp.concatenate([a, b], axis=1)


def pick(mask, x):
    x = x if x.dtype == jnp.bfloat16 else split(x)
    y = jnp.dot(mask, x, preferred_element_type=jnp.float32)
    return y[:, :LANES] + y[:, LANES:]


def flip(i, k, n):
    if n & (n - 1):
        return None
    both, bit = 0, 1
    while bit < n:
        if k & bit:
            both = both + bit * lax.rem(i // bit, 2)
        bit *= 2
    return i + k - 2 * both


def offsets(n):
    return sorted(range(1, n), key=lambda k: bin(k).count("1"))


def east_of(x):
    return pltpu.roll(x, x.shape[1] - 1, 1)


def south_of(x):
    return pltpu.roll(x, x.shape[0] - 1, 0)


def face(eta, eta_next, base, coef, q):
    depth = jnp.maximum(eta, eta_next) - base
    driving = (GRAVITY * TIME_STEP / CELL_WIDTH) * jnp.maximum(depth, 0.0) * (eta_next - eta)
    power = jnp.exp2(jnp.log2(jnp.maximum(depth, DEPTH_FLOOR)) * (-7.0 / 3.0))
    damping = 1.0 + coef * jnp.abs(q) * power
    return jnp.where(coef > 0.0, (q - driving) / damping, 0.0)


def kernel(
    nx, ny, cap,
    depth_in, bed_in, east_in, south_in, rough_in, wet_in, soil_in, rain_in, col_in, blk_in,
    h, qe, qs, newsoil,
    bed, fric, rough, wet, land_in, index,
    tile_face, rim, rim_face, flank, flank_face,
    give, take, give_idx, take_idx, give_lev, take_lev,
    st_rows, st_cols, st_corner, st_in_rows, st_in_cols, st_in_corner,
    h_rows, h_cols, h_in_rows, h_in_cols, h_in_corner,
    place, place_t, where_to, where_to_t, from_row, from_col, at_end, give_edge, take_edge, span,
    in_sem, give_r, lev_r, edge_r, data_s, idx_s, idx_r, st_s, st_r, hs_s, hs_r,
):
    gx, gy = lax.axis_index("gx"), lax.axis_index("gy")
    tr, tc = rough.shape
    land = land_in.shape[1]
    chunks = tc // LANES

    loads = [
        pltpu.make_async_copy(src, dst, in_sem.at[i])
        for i, src, dst in [
            (0, col_in, index.at[0]), (0, blk_in, index.at[1]),
            (1, soil_in, land_in.at[0]), (1, rain_in, land_in.at[1]),
            (2, rough_in, rough), (2, wet_in, wet), (2, bed_in, bed),
            (2, east_in, qe), (2, south_in, qs), (3, depth_in, h),
        ]
    ]
    for c in loads:
        c.start()

    def settle(sem, tiles):
        ref = span.at[pl.ds(0, tiles)]
        pltpu.make_async_copy(ref, ref, sem).wait()

    def there(k):
        dx, dy = AROUND[k]
        x, y = gx + dx, gy + dy
        return (x >= 0) & (x < nx) & (y >= 0) & (y < ny)

    barrier = pltpu.get_barrier_semaphore()
    for k in range(1, ny):
        pl.semaphore_signal(
            barrier, inc=1, device_id=(gx, lax.rem(gy + k, ny)), device_id_type=MESH
        )
    total = ny - 1
    for k in (NW, N, NE, SW, S, SE):
        dx, dy = AROUND[k]

        @pl.when(there(k))
        def _(dx=dx, dy=dy):
            pl.semaphore_signal(barrier, inc=1, device_id=(gx + dx, gy + dy), device_id_type=MESH)

        total = total + there(k).astype(jnp.int32)

    for k, ref in ((N, (st_in_rows, h_in_rows)), (S, (st_in_rows, h_in_rows))):
        @pl.when(jnp.logical_not(there(k)))
        def _(k=k, ref=ref):
            for r in ref:
                r[int(k == S)] = jnp.zeros(r.shape[1:], r.dtype)
    for k, ref in ((W, (st_in_cols, h_in_cols)), (E, (st_in_cols, h_in_cols))):
        @pl.when(jnp.logical_not(there(k)))
        def _(k=k, ref=ref):
            for r in ref:
                r[int(k == E)] = jnp.zeros(r.shape[1:], r.dtype)
    for n, k in enumerate((NW, NE, SW, SE)):
        @pl.when(jnp.logical_not(there(k)))
        def _(n=n):
            for r in (st_in_corner, h_in_corner):
                r[n] = jnp.zeros(r.shape[1:], r.dtype)

    def to_peer(k):
        if k == 0:
            return gy
        peer = flip(gy, k, ny)
        return lax.rem(gy + k, ny) if peer is None else peer

    def from_peer(k):
        peer = flip(gy, k, ny)
        return lax.rem(gy + ny - k, ny) if peer is None else peer

    def send(src, dst, ss, rs, peer):
        pltpu.make_async_remote_copy(
            src_ref=src, dst_ref=dst, send_sem=ss, recv_sem=rs,
            device_id=(gx, peer), device_id_type=MESH,
        ).start()

    def arrive(dst, rs):
        pltpu.make_async_copy(dst, dst, rs).wait()

    pltpu.make_async_copy(index, index, in_sem.at[0]).wait()
    column = index[0]
    groups = max(EDGE, ny)
    is_col = lax.broadcasted_iota(jnp.int32, (groups, land), 0) == column
    before = lax.broadcasted_iota(jnp.int32, (land, land), 0) < lax.broadcasted_iota(
        jnp.int32, (land, land), 1
    )
    rank = jnp.dot(
        is_col.astype(jnp.float32).astype(jnp.bfloat16),
        before.astype(jnp.float32).astype(jnp.bfloat16),
        preferred_element_type=jnp.float32,
    )
    rank = jnp.sum(jnp.where(is_col, rank, 0.0), axis=0, keepdims=True)
    slot = column.astype(jnp.float32) * cap + rank

    block = index[1].astype(jnp.float32)
    row = jnp.floor((block + 0.5) * (1.0 / chunks))
    chunk = block - row * chunks
    line = lax.broadcasted_iota(jnp.int32, (EDGE, land), 0)
    code = jnp.where(line == 0, row + 1.0, jnp.where(line == 1, chunk, 0.0))
    code = code.astype(jnp.bfloat16)
    seat = lax.broadcasted_iota(jnp.int32, (cap, land), 0).astype(jnp.float32)

    pltpu.make_async_copy(land_in, land_in, in_sem.at[1]).wait()
    runoff = split(land_in[1] * land_in[0] * land_in[0])

    def pack(k):
        hit = (seat == slot - (to_peer(k) * cap).astype(jnp.float32)).astype(jnp.float32)
        mask = hit.astype(jnp.bfloat16)
        place[k] = mask
        owner = lax.dot_general(
            code, mask, (((1,), (1,)), ((), ())), preferred_element_type=jnp.float32
        )
        give_idx[k] = owner[1:2] * tr + owner[0:1] - 1.0
        give[k] = pick(mask, runoff)

    for n, k in enumerate(offsets(ny)):
        pack(k)
        if n == 0:
            pl.semaphore_wait(barrier, total)
        send(give_idx.at[k], take_idx.at[k], idx_s, idx_r, to_peer(k))
        send(give.at[k], take.at[k], data_s, give_r.at[k - 1], to_peer(k))
    pack(0)
    take_idx[0] = give_idx[0]

    settle(in_sem.at[2], 5 * tr * tc // (EDGE * LANES))
    kind = rough[...]
    f = jnp.zeros((tr, tc), jnp.float32)
    for i, coefficient in enumerate(MANNING):
        f = jnp.where(kind == i, coefficient * coefficient, f)
    fric[...] = jnp.where(wet[...] > 0, f, -1.0)
    lane_low = lax.broadcasted_iota(jnp.int32, (tr, LANES), 1) < LANES // 2
    low8 = lane_low[:EDGE]
    sub_low = lax.broadcasted_iota(jnp.int32, (EDGE, 1), 0) < EDGE // 2
    half_turn = lambda x: pltpu.roll(x, EDGE // 2, 0)
    first, last = pl.ds(0, LANES), pl.ds(tc - LANES, LANES)

    def ends_of(ref):
        ends = jnp.where(lane_low, ref[0:tr, 0:LANES], ref[0:tr, tc - LANES : tc]).T
        return ends[0:EDGE], ends[LANES - EDGE :]

    pairs = ((bed, fric), (qe, qs))
    for i, (a, b) in enumerate(pairs):
        st_rows[0, i] = jnp.where(sub_low, a[0:EDGE, 0:tc], half_turn(b[0:EDGE, 0:tc]))
        st_rows[1, i] = jnp.where(
            sub_low, half_turn(b[tr - EDGE : tr, 0:tc]), a[tr - EDGE : tr, 0:tc]
        )
        (aw, ae), (bw, be) = ends_of(a), ends_of(b)
        st_cols[0, i] = jnp.where(sub_low, aw, half_turn(bw))
        st_cols[1, i] = jnp.where(sub_low, half_turn(be), ae)
    for dx in range(2):
        x, y = st_rows[dx, 0, :, first], st_rows[dx, 1, :, first]
        st_corner[dx, 0] = jnp.where(low8, x, pltpu.roll(y, LANES // 2, 1))
        x, y = st_rows[dx, 0, :, last], st_rows[dx, 1, :, last]
        st_corner[dx, 1] = jnp.where(low8, pltpu.roll(y, LANES // 2, 1), x)

    def edges(piece, tiles, ss, rs):
        def start():
            for k in (NW, NE, SW, SE, W, E, N, S):
                @pl.when(there(k))
                def _(k=k):
                    dx, dy = AROUND[k]
                    src, dst = piece(k)
                    pltpu.make_async_remote_copy(
                        src_ref=src, dst_ref=dst, send_sem=ss, recv_sem=rs,
                        device_id=(gx + dx, gy + dy), device_id_type=MESH,
                    ).start()

        def wait(sem):
            up = (gx > 0).astype(jnp.int32) + (gx < nx - 1).astype(jnp.int32)
            side = (gy > 0).astype(jnp.int32) + (gy < ny - 1).astype(jnp.int32)
            for r in range(3):
                for c in range(3):
                    n = r * tiles[0] + c * tiles[1] + r * c * tiles[2]
                    if n:
                        @pl.when((up == r) & (side == c))
                        def _(n=n):
                            settle(sem, n)

        return start, lambda: wait(rs), lambda: wait(ss)

    corner_at = {NW: 3, NE: 2, SW: 1, SE: 0}

    def st_piece(k):
        dx, dy = AROUND[k]
        if dy == 0:
            return st_rows.at[int(dx > 0)], st_in_rows.at[int(dx < 0)]
        if dx == 0:
            return st_cols.at[int(dy > 0)], st_in_cols.at[int(dy < 0)]
        return st_corner.at[int(dx > 0), int(dy > 0)], st_in_corner.at[corner_at[k]]

    def h_piece(k):
        dx, dy = AROUND[k]
        if dy == 0:
            return h_rows.at[int(dx > 0)], h_in_rows.at[int(dx < 0)]
        if dx == 0:
            return h_cols.at[int(dy > 0)], h_in_cols.at[int(dy < 0)]
        side = last if dy > 0 else first
        return h_rows.at[int(dx > 0), :, side], h_in_corner.at[corner_at[k]]

    st_start, st_wait, st_done = edges(
        st_piece, (2 * chunks, 2 * (tr // LANES), 1), st_s, st_r
    )
    h_start, h_wait, h_done = edges(h_piece, (chunks, tr // LANES, 1), hs_s, hs_r)
    st_start()

    lane = lax.broadcasted_iota(jnp.int32, (tr, LANES), 1)
    own = lane < LANES // 2

    def keep(x, i):
        rim[i, 0:EDGE] = x[tr - EDGE : tr, 0:tc]
        rim[i, 2 * EDGE : 3 * EDGE] = x[0:EDGE, 0:tc]
        flank[i, 0:tr] = jnp.where(
            lane < LANES // 4,
            x[0:tr, 0:LANES],
            pltpu.roll(x[0:tr, tc - LANES : tc], LANES // 2, 1),
        )

    def faces(b, fr, out):
        b_e, f_e, b_s, f_s = east_of(b), east_of(fr), south_of(b), south_of(fr)
        half = 0.5 * GRAVITY * TIME_STEP
        out[0] = jnp.maximum(b, b_e)
        out[1] = jnp.maximum(b, b_s)
        out[2] = jnp.where((fr > 0.0) & (f_e > 0.0), half * (fr + f_e), -1.0)
        out[3] = jnp.where((fr > 0.0) & (f_s > 0.0), half * (fr + f_s), -1.0)

    def substep(depth, b, e, s, out):
        eta = depth + b
        e = face(eta, east_of(eta), out[0], out[2], e)
        s = face(eta, south_of(eta), out[1], out[3], s)
        depth = depth + (TIME_STEP / CELL_WIDTH) * (
            pltpu.roll(e, 1, 1) - e + pltpu.roll(s, 1, 0) - s
        )
        return depth, e, s

    for i, x in enumerate((bed, fric, qe, qs)):
        keep(x, i)
    faces(bed[...], fric[...], tile_face)

    reach = EDGE // 2
    turn_of = jnp.zeros((1, land), jnp.float32)
    for k in range(1, ny):
        turn_of = jnp.where(column == to_peer(k), 1.0 * k, turn_of)
    outer = (row < reach) | (row >= tr - reach)
    line = jnp.where(row < reach, row, row - (tr - EDGE))
    key = jnp.where(outer, (turn_of * chunks + chunk) * EDGE + line, -1.0)

    def one_hot(rows, key):
        line = lax.broadcasted_iota(jnp.int32, (rows, land), 0).astype(jnp.float32)
        return (line == key).astype(jnp.float32).T.astype(jnp.bfloat16)

    from_row[...] = one_hot(ny * chunks * EDGE, key)
    head, tail = chunk == 0.0, chunk == chunks - 1.0
    key = jnp.where((head | tail) & jnp.logical_not(outer), row, -1.0)
    for k in range(ny):
        from_col[k] = one_hot(tr, jnp.where(turn_of == k, key, -1.0))
    line = lax.broadcasted_iota(jnp.int32, (LANES, land), 0)
    ends = ((line < reach) & head) | ((line >= LANES - reach) & tail)
    at_end[...] = ends.astype(jnp.float32).T

    for d in range(ny):
        place_t[d] = place[d].astype(jnp.float32).T.astype(jnp.bfloat16)

    settle_idx = take_idx.at[pl.ds(1, ny - 1)]
    if ny > 1:
        arrive(settle_idx, idx_r)
    line = lax.broadcasted_iota(jnp.int32, (land, cap), 0).astype(jnp.float32)
    for d in range(ny):
        target = (line == take_idx[d]).astype(jnp.float32)
        where_to[d] = target.astype(jnp.bfloat16)
        where_to_t[d] = target.T.astype(jnp.bfloat16)

    pltpu.make_async_copy(depth_in, h, in_sem.at[3]).wait()
    inflow = pick(where_to[0], give[0])
    for k in offsets(ny):
        arrive(take.at[k], give_r.at[k - 1])
        inflow = inflow + pick(where_to[k], take[k])
    for c in range(chunks):
        at = (pl.ds(0, tr), pl.ds(c * LANES, LANES))
        h[at] = h[at] + inflow[c * tr : (c + 1) * tr]

    h_rows[0] = h[0:EDGE, 0:tc]
    h_rows[1] = h[tr - EDGE : tr, 0:tc]
    h_cols[0], h_cols[1] = ends_of(h)
    h_start()
    keep(h, 4)

    for step in range(SUB):
        h[...], qe[...], qs[...] = substep(h[...], bed[...], qe[...], qs[...], tile_face)

    high = lax.broadcasted_iota(jnp.int32, (tr, LANES), 0)
    within = (high >= reach) & (high < tr - reach)
    blocks = []
    for c in range(chunks):
        inside = within
        if c == 0:
            inside = inside & (lane >= reach)
        if c == chunks - 1:
            inside = inside & (lane < LANES - reach)
        blocks.append(jnp.where(inside, h[:, c * LANES : (c + 1) * LANES], 0.0))
    blocks = split(jnp.concatenate(blocks, axis=0))
    for k in offsets(ny):
        give_lev[k] = pick(where_to_t[k], blocks)
        send(give_lev.at[k], take_lev.at[k], data_s, lev_r.at[k - 1], from_peer(k))
    take_lev[0] = pick(where_to_t[0], blocks)

    gap = jnp.zeros((LANES // 2 - 2 * EDGE, tr), jnp.float32)
    half_gap = jnp.zeros((LANES // 2, tr), jnp.float32)
    lane8 = lane[:EDGE]

    def wrap(i, halo, west, east, corner_w, corner_e):
        side = jnp.concatenate([half_gap, east, gap, west], axis=0)
        rim[i, EDGE : 2 * EDGE] = halo
        flank[i, 0:tr] = jnp.where(own, flank[i, 0:tr], side.T)
        corner = jnp.where(lane8 < 3 * LANES // 4, corner_e, corner_w)
        far = pltpu.roll(halo[:, tc - LANES :], LANES // 2, 1)
        line = jnp.where(lane8 < LANES // 4, halo[:, :LANES], far)
        flank[i, tr : tr + EDGE] = jnp.where(low8, line, corner)

    def turn(x):
        return pltpu.roll(x, LANES // 2, 1)

    st_wait()
    nw, ne, sw, se = [st_in_corner[n] for n in range(4)]
    west_a, west_b = jnp.where(sub_low, sw, nw), half_turn(jnp.where(sub_low, nw, sw))
    east_a, east_b = jnp.where(sub_low, se, ne), half_turn(jnp.where(sub_low, ne, se))
    for i in range(2):
        up, down = st_in_rows[0, i], st_in_rows[1, i]
        west, east = st_in_cols[0, i], st_in_cols[1, i]
        cw = (west_a, west_b) if i == 0 else (turn(west_a), turn(west_b))
        ce = (turn(east_a), turn(east_b)) if i == 0 else (east_a, east_b)
        wrap(2 * i, jnp.where(sub_low, down, up), west, east, cw[0], ce[0])
        wrap(
            2 * i + 1, half_turn(jnp.where(sub_low, up, down)), half_turn(west),
            half_turn(east), cw[1], ce[1],
        )
    faces(rim[0], rim[1], rim_face)
    faces(flank[0], flank[1], flank_face)

    h_wait()
    nw, ne, sw, se = [h_in_corner[n] for n in range(4)]
    wrap(
        4, jnp.where(sub_low, h_in_rows[1], h_in_rows[0]), h_in_cols[0], h_in_cols[1],
        jnp.where(sub_low, sw, nw), turn(jnp.where(sub_low, se, ne)),
    )

    for step in range(SUB):
        for x, out in ((rim, rim_face), (flank, flank_face)):
            x[4], x[2], x[3] = substep(x[4], x[0], x[2], x[3], out)

    def merge(i, x):
        x[0:EDGE] = jnp.where(sub_low, rim[i, 2 * EDGE : 3 * EDGE], x[0:EDGE])
        x[tr - EDGE : tr] = jnp.where(sub_low, x[tr - EDGE : tr], rim[i, 0:EDGE])
        edge = flank[i, 0:tr]
        x[:, 0:LANES] = jnp.where(lane < reach, edge, x[:, 0:LANES])
        x[:, tc - LANES : tc] = jnp.where(
            lane >= LANES - reach, turn(edge), x[:, tc - LANES : tc]
        )

    merge(4, h)
    give_edge[:, 0:tc] = jnp.where(sub_low, h[0:EDGE], h[tr - EDGE : tr])
    west, east = ends_of(h)
    give_edge[:, tc : tc + tr] = jnp.where(sub_low, west, east)
    for k in offsets(ny):
        send(give_edge, take_edge.at[k], data_s, edge_r, from_peer(k))
    take_edge[0] = give_edge[...]
    merge(2, qe)
    merge(3, qs)
    mine = pick(place_t[0], take_lev[0])
    for k in offsets(ny):
        arrive(take_lev.at[k], lev_r.at[k - 1])
        mine = mine + pick(place_t[k], take_lev[k])
    if ny > 1:
        arrive(take_edge.at[pl.ds(1, ny - 1)], edge_r)
    table = [
        take_edge[k, :, c * LANES : (c + 1) * LANES] for k in range(ny) for c in range(chunks)
    ]
    mine = mine + pick(from_row[...], jnp.concatenate(table, axis=0))
    blank = jnp.zeros((LANES - 2 * EDGE, tr), jnp.float32)
    sides = jnp.zeros((land, LANES), jnp.float32)
    for k in range(ny):
        side = take_edge[k, :, tc : tc + tr]
        sides = sides + pick(from_col[k], jnp.concatenate([side, blank, side], axis=0).T)
    mine = mine + at_end[...] * sides
    store, rain = land_in[0], land_in[1]
    runoff = rain * store * store
    newsoil[...] = (
        store + rain - runoff + INFIL_RATE * (1.0 - store) * (1.0 - jnp.exp(-mine))
    )
    if ny > 1:
        arrive(settle_idx, idx_s)
        settle(data_s, (ny - 1) * (2 * cap // EDGE + (tc + tr) // LANES))
    st_done()
    h_done()


def write_out(h, qe, qs, newsoil, depth_out, east_out, south_out, soil_out, sem):
    copies = [
        pltpu.make_async_copy(src, dst, sem.at[i])
        for i, (src, dst) in enumerate(
            [
                (h, depth_out), (qe, east_out), (qs, south_out), (newsoil, soil_out),
            ]
        )
    ]
    for c in copies:
        c.start()
    for c in copies:
        c.wait()


def local(depth, bed, east, south, rough, wet, soil, rain, column, block):
    nx, ny = lax.axis_size("gx"), lax.axis_size("gy")
    tr, tc = depth.shape
    land = soil.shape[1]
    cap = 2 * land // ny
    grid = (tr, tc)
    rim, flank = (3 * EDGE, tc), (tr + EDGE, LANES)
    f32, bf16, i32 = jnp.float32, jnp.bfloat16, jnp.int32
    v = pltpu.VMEM
    dma = pltpu.SemaphoreType.DMA
    peers = max(1, ny - 1)

    def edge_bufs(k):
        return [v((2, *k, EDGE, tc), f32), v((2, *k, EDGE, tr), f32)]

    corners = v((2, 2, EDGE, LANES), f32)
    in_corners = v((4, EDGE, LANES), f32)
    span = max(5 * tr * tc, peers * (2 * cap * LANES + EDGE * (tc + tr)), 4 * EDGE * (2 * tc + 2 * tr + 4 * LANES))
    any_ = pl.BlockSpec(memory_space=pltpu.MemorySpace.HBM)
    vmem = pl.BlockSpec(memory_space=pltpu.VMEM)
    shape = jax.ShapeDtypeStruct
    out = pl.pallas_call(
        functools.partial(kernel, nx, ny, cap),
        out_shape=[shape(grid, f32)] * 3 + [shape((land, LANES), f32)],
        in_specs=[any_] * 10,
        out_specs=[vmem] * 4,
        scratch_shapes=[v(grid, f32)] * 2
        + [v((tr, tc), i32)] * 2
        + [v((2, land, LANES), f32), v((2, 1, land), i32)]
        + [v((4, *grid), f32), v((5, *rim), f32), v((4, *rim), f32)]
        + [v((5, *flank), f32), v((4, *flank), f32)]
        + [v((ny, cap, LANES), f32)] * 2
        + [v((ny, 1, cap), f32)] * 2
        + [v((ny, cap, LANES), f32)] * 2
        + edge_bufs((2,)) + [corners] + edge_bufs((2,)) + [in_corners]
        + edge_bufs(()) + edge_bufs(()) + [in_corners]
        + [v((ny, cap, land), bf16), v((ny, land, cap), bf16)]
        + [v((ny, land, cap), bf16), v((ny, cap, land), bf16)]
        + [v((land, ny * (tc // LANES) * EDGE), bf16), v((ny, land, tr), bf16), v((land, LANES), f32)]
        + [v((EDGE, tc + tr), f32), v((ny, EDGE, tc + tr), f32)]
        + [v((span // (EDGE * LANES), EDGE, LANES), f32)]
        + [dma((4,))]
        + [dma((peers,))] * 2
        + [dma] * 8,
        compiler_params=pltpu.CompilerParams(collective_id=0, has_side_effects=True, vmem_limit_bytes=24 << 20
        ),
    )(
        *(
            pltpu.with_memory_space_constraint(x, pltpu.MemorySpace.HBM)
            for x in (
                depth, bed, east, south, rough, wet, soil[0], rain[0],
                column.reshape(1, land), block,
            )
        )
    )
    out = pl.pallas_call(
        write_out,
        out_shape=[shape((tr, tc), f32)] * 3 + [shape((land, LANES), f32)],
        in_specs=[vmem] * 4,
        out_specs=[any_] * 4,
        scratch_shapes=[dma((4,))],
        compiler_params=pltpu.CompilerParams(vmem_limit_bytes=8 << 20),
    )(*out)
    return out[0], out[1], out[2], out[3][None]


def solution(mesh):
    grid = P("gx", "gy")
    blocks = P("gx", "gy", None)
    return jax.shard_map(
        local, mesh=mesh,
        in_specs=(grid,) * 6 + (blocks,) * 3 + (grid,),
        out_specs=(grid,) * 3 + (blocks,),
        check_vma=False,
    )
```

```python
import functools

import jax
import jax.numpy as jnp
from jax import lax
from jax.experimental import pallas as pl
from jax.experimental.pallas import tpu as pltpu
from jax.sharding import PartitionSpec as P

SUB = 4
GRAVITY = 9.81
TIME_STEP = 1.0
CELL_WIDTH = 30.0
DEPTH_FLOOR = 0.3
INFIL_RATE = 0.5
MANNING = (0.02, 0.03, 0.035, 0.045, 0.06, 0.08, 0.1, 0.15)
POWER = -7.0 / 3.0
STRIDE = TIME_STEP / CELL_WIDTH
DEEP = GRAVITY * STRIDE * STRIDE
FLOW = DEEP * STRIDE
DRAG = 0.5 * GRAVITY * TIME_STEP * DEEP ** (-POWER) / FLOW
LANES = 128
EDGE = 8
MESH = pl.DeviceIdType.MESH
AROUND = ((-1, -1), (-1, 0), (-1, 1), (0, -1), (0, 1), (1, -1), (1, 0), (1, 1))
NW, N, NE, W, E, SW, S, SE = range(8)


def split(x):
    a = x.astype(jnp.bfloat16)
    b = (x - a.astype(jnp.float32)).astype(jnp.bfloat16)
    return jnp.concatenate([a, b], axis=1)


def pick(mask, x):
    x = x if x.dtype == jnp.bfloat16 else split(x)
    y = jnp.dot(mask, x, preferred_element_type=jnp.float32)
    return y[:, :LANES] + y[:, LANES:]


def flip(i, k, n):
    if n & (n - 1):
        return None
    both, bit = 0, 1
    while bit < n:
        if k & bit:
            both = both + bit * lax.rem(i // bit, 2)
        bit *= 2
    return i + k - 2 * both


def offsets(n):
    return sorted(range(1, n), key=lambda k: bin(k).count("1"))


def east_of(x):
    return pltpu.roll(x, x.shape[1] - 1, 1)


def south_of(x):
    return pltpu.roll(x, x.shape[0] - 1, 0)


def face(eta, eta_next, base, coef, closed, q):
    depth = jnp.maximum(eta, eta_next) - base
    driving = jnp.maximum(depth, 0.0) * (eta_next - eta)
    power = jnp.exp2(jnp.log2(jnp.maximum(depth, DEEP * DEPTH_FLOOR)) * POWER)
    return (q - driving) / (closed + coef * jnp.abs(q) * power)


def kernel(
    nx, ny, cap,
    depth_in, bed_in, east_in, south_in, rough_in, wet_in, soil_in, rain_in, col_in, blk_in,
    h, qe, qs, dry, gain, mine, edge, from_row, from_col, at_end,
    bed, fric, rough, wet, land_in, index,
    tile_face, rim, rim_face, flank, flank_face,
    give, take, give_idx, take_idx, give_lev, take_lev,
    st_rows, st_cols, st_corner, st_in_rows, st_in_cols, st_in_corner,
    h_rows, h_cols, h_in_rows, h_in_cols, h_in_corner,
    place, place_t, where_to, where_to_t, give_edge, take_edge, span,
    in_sem, give_r, lev_r, edge_r, data_s, idx_s, idx_r, st_s, st_r, hs_s, hs_r,
):
    gx, gy = lax.axis_index("gx"), lax.axis_index("gy")
    tr, tc = rough.shape
    land = land_in.shape[1]
    chunks = tc // LANES

    loads = [
        pltpu.make_async_copy(src, dst, in_sem.at[i])
        for i, src, dst in [
            (0, col_in, index.at[0]), (0, blk_in, index.at[1]),
            (1, soil_in, land_in.at[0]), (1, rain_in, land_in.at[1]),
            (2, rough_in, rough), (2, wet_in, wet), (2, bed_in, bed),
            (2, east_in, qe), (2, south_in, qs), (3, depth_in, h),
        ]
    ]
    for c in loads:
        c.start()

    def settle(sem, tiles):
        ref = span.at[pl.ds(0, tiles)]
        pltpu.make_async_copy(ref, ref, sem).wait()

    def there(k):
        dx, dy = AROUND[k]
        x, y = gx + dx, gy + dy
        return (x >= 0) & (x < nx) & (y >= 0) & (y < ny)

    barrier = pltpu.get_barrier_semaphore()
    for k in range(1, ny):
        pl.semaphore_signal(
            barrier, inc=1, device_id=(gx, lax.rem(gy + k, ny)), device_id_type=MESH
        )
    total = ny - 1
    for k in (NW, N, NE, SW, S, SE):
        dx, dy = AROUND[k]

        @pl.when(there(k))
        def _(dx=dx, dy=dy):
            pl.semaphore_signal(barrier, inc=1, device_id=(gx + dx, gy + dy), device_id_type=MESH)

        total = total + there(k).astype(jnp.int32)

    for k, ref in ((N, (st_in_rows, h_in_rows)), (S, (st_in_rows, h_in_rows))):
        @pl.when(jnp.logical_not(there(k)))
        def _(k=k, ref=ref):
            for r in ref:
                r[int(k == S)] = jnp.zeros(r.shape[1:], r.dtype)
    for k, ref in ((W, (st_in_cols, h_in_cols)), (E, (st_in_cols, h_in_cols))):
        @pl.when(jnp.logical_not(there(k)))
        def _(k=k, ref=ref):
            for r in ref:
                r[int(k == E)] = jnp.zeros(r.shape[1:], r.dtype)
    for n, k in enumerate((NW, NE, SW, SE)):
        @pl.when(jnp.logical_not(there(k)))
        def _(n=n):
            for r in (st_in_corner, h_in_corner):
                r[n] = jnp.zeros(r.shape[1:], r.dtype)

    def to_peer(k):
        if k == 0:
            return gy
        peer = flip(gy, k, ny)
        return lax.rem(gy + k, ny) if peer is None else peer

    def from_peer(k):
        peer = flip(gy, k, ny)
        return lax.rem(gy + ny - k, ny) if peer is None else peer

    def send(src, dst, ss, rs, peer):
        pltpu.make_async_remote_copy(
            src_ref=src, dst_ref=dst, send_sem=ss, recv_sem=rs,
            device_id=(gx, peer), device_id_type=MESH,
        ).start()

    def arrive(dst, rs):
        pltpu.make_async_copy(dst, dst, rs).wait()

    pltpu.make_async_copy(index, index, in_sem.at[0]).wait()
    column = index[0]
    groups = max(EDGE, ny)
    is_col = lax.broadcasted_iota(jnp.int32, (groups, land), 0) == column
    before = lax.broadcasted_iota(jnp.int32, (land, land), 0) < lax.broadcasted_iota(
        jnp.int32, (land, land), 1
    )
    rank = jnp.dot(
        is_col.astype(jnp.float32).astype(jnp.bfloat16),
        before.astype(jnp.float32).astype(jnp.bfloat16),
        preferred_element_type=jnp.float32,
    )
    rank = jnp.sum(jnp.where(is_col, rank, 0.0), axis=0, keepdims=True)
    slot = column.astype(jnp.float32) * cap + rank

    block = index[1].astype(jnp.float32)
    row = jnp.floor((block + 0.5) * (1.0 / chunks))
    chunk = block - row * chunks
    line = lax.broadcasted_iota(jnp.int32, (EDGE, land), 0)
    code = jnp.where(line == 0, row + 1.0, jnp.where(line == 1, chunk, 0.0))
    code = code.astype(jnp.bfloat16)
    seat = lax.broadcasted_iota(jnp.int32, (cap, land), 0).astype(jnp.float32)

    pltpu.make_async_copy(land_in, land_in, in_sem.at[1]).wait()
    runoff = split(land_in[1] * land_in[0] * land_in[0])

    def pack(k):
        hit = (seat == slot - (to_peer(k) * cap).astype(jnp.float32)).astype(jnp.float32)
        mask = hit.astype(jnp.bfloat16)
        place[k] = mask
        owner = lax.dot_general(
            code, mask, (((1,), (1,)), ((), ())), preferred_element_type=jnp.float32
        )
        give_idx[k] = owner[1:2] * tr + owner[0:1] - 1.0
        give[k] = pick(mask, runoff)

    for n, k in enumerate(offsets(ny)):
        pack(k)
        if n == 0:
            pl.semaphore_wait(barrier, total)
        send(give_idx.at[k], take_idx.at[k], idx_s, idx_r, to_peer(k))
        send(give.at[k], take.at[k], data_s, give_r.at[k - 1], to_peer(k))
    pack(0)
    take_idx[0] = give_idx[0]

    settle(in_sem.at[2], 5 * tr * tc // (EDGE * LANES))
    bed[...] = bed[...] * DEEP
    qe[...] = qe[...] * FLOW
    qs[...] = qs[...] * FLOW
    kind = rough[...]
    f = jnp.zeros((tr, tc), jnp.float32)
    for i, coefficient in enumerate(MANNING):
        f = jnp.where(kind == i, coefficient * coefficient, f)
    fric[...] = jnp.where(wet[...] > 0, f, -1.0)
    lane_low = lax.broadcasted_iota(jnp.int32, (tr, LANES), 1) < LANES // 2
    low8 = lane_low[:EDGE]
    sub_low = lax.broadcasted_iota(jnp.int32, (EDGE, 1), 0) < EDGE // 2
    half_turn = lambda x: pltpu.roll(x, EDGE // 2, 0)
    first, last = pl.ds(0, LANES), pl.ds(tc - LANES, LANES)

    def ends_of(ref):
        ends = jnp.where(lane_low, ref[0:tr, 0:LANES], ref[0:tr, tc - LANES : tc]).T
        return ends[0:EDGE], ends[LANES - EDGE :]

    pairs = ((bed, fric), (qe, qs))
    for i, (a, b) in enumerate(pairs):
        st_rows[0, i] = jnp.where(sub_low, a[0:EDGE, 0:tc], half_turn(b[0:EDGE, 0:tc]))
        st_rows[1, i] = jnp.where(
            sub_low, half_turn(b[tr - EDGE : tr, 0:tc]), a[tr - EDGE : tr, 0:tc]
        )
        (aw, ae), (bw, be) = ends_of(a), ends_of(b)
        st_cols[0, i] = jnp.where(sub_low, aw, half_turn(bw))
        st_cols[1, i] = jnp.where(sub_low, half_turn(be), ae)
    for dx in range(2):
        x, y = st_rows[dx, 0, :, first], st_rows[dx, 1, :, first]
        st_corner[dx, 0] = jnp.where(low8, x, pltpu.roll(y, LANES // 2, 1))
        x, y = st_rows[dx, 0, :, last], st_rows[dx, 1, :, last]
        st_corner[dx, 1] = jnp.where(low8, pltpu.roll(y, LANES // 2, 1), x)

    def edges(piece, tiles, ss, rs):
        def start():
            for k in (NW, NE, SW, SE, W, E, N, S):
                @pl.when(there(k))
                def _(k=k):
                    dx, dy = AROUND[k]
                    src, dst = piece(k)
                    pltpu.make_async_remote_copy(
                        src_ref=src, dst_ref=dst, send_sem=ss, recv_sem=rs,
                        device_id=(gx + dx, gy + dy), device_id_type=MESH,
                    ).start()

        def wait(sem):
            up = (gx > 0).astype(jnp.int32) + (gx < nx - 1).astype(jnp.int32)
            side = (gy > 0).astype(jnp.int32) + (gy < ny - 1).astype(jnp.int32)
            for r in range(3):
                for c in range(3):
                    n = r * tiles[0] + c * tiles[1] + r * c * tiles[2]
                    if n:
                        @pl.when((up == r) & (side == c))
                        def _(n=n):
                            settle(sem, n)

        return start, lambda: wait(rs), lambda: wait(ss)

    corner_at = {NW: 3, NE: 2, SW: 1, SE: 0}

    def st_piece(k):
        dx, dy = AROUND[k]
        if dy == 0:
            return st_rows.at[int(dx > 0)], st_in_rows.at[int(dx < 0)]
        if dx == 0:
            return st_cols.at[int(dy > 0)], st_in_cols.at[int(dy < 0)]
        return st_corner.at[int(dx > 0), int(dy > 0)], st_in_corner.at[corner_at[k]]

    def h_piece(k):
        dx, dy = AROUND[k]
        if dy == 0:
            return h_rows.at[int(dx > 0)], h_in_rows.at[int(dx < 0)]
        if dx == 0:
            return h_cols.at[int(dy > 0)], h_in_cols.at[int(dy < 0)]
        side = last if dy > 0 else first
        return h_rows.at[int(dx > 0), :, side], h_in_corner.at[corner_at[k]]

    st_start, st_wait, st_done = edges(
        st_piece, (2 * chunks, 2 * (tr // LANES), 1), st_s, st_r
    )
    h_start, h_wait, h_done = edges(h_piece, (chunks, tr // LANES, 1), hs_s, hs_r)

    lane = lax.broadcasted_iota(jnp.int32, (tr, LANES), 1)
    own = lane < LANES // 2

    def keep(x, i):
        rim[i, 0:EDGE] = x[tr - EDGE : tr, 0:tc]
        rim[i, 2 * EDGE : 3 * EDGE] = x[0:EDGE, 0:tc]
        flank[i, 0:tr] = jnp.where(
            lane < LANES // 4,
            x[0:tr, 0:LANES],
            pltpu.roll(x[0:tr, tc - LANES : tc], LANES // 2, 1),
        )

    def faces(b, fr, out):
        b_e, f_e, b_s, f_s = east_of(b), east_of(fr), south_of(b), south_of(fr)
        out[0] = jnp.maximum(b, b_e)
        out[1] = jnp.maximum(b, b_s)
        for i, other in ((2, f_e), (3, f_s)):
            is_open = (fr > 0.0) & (other > 0.0)
            out[i] = jnp.where(is_open, DRAG * (fr + other), 0.0)
            out[i + 2] = jnp.where(is_open, 1.0, jnp.inf)

    def substep(step, h, b, e, s, out):
        eta = h[...] + b[...] if step == 0 else h[...]
        east = face(eta, east_of(eta), out[0], out[2], out[4], e[...])
        south = face(eta, south_of(eta), out[1], out[3], out[5], s[...])
        e[...] = east
        s[...] = south
        eta = eta + (pltpu.roll(east, 1, 1) - east + pltpu.roll(south, 1, 0) - south)
        h[...] = eta - b[...] if step == SUB - 1 else eta

    for i, x in enumerate((bed, fric, qe, qs)):
        keep(x, i)
    faces(bed[...], fric[...], tile_face)

    reach = EDGE // 2
    turn_of = jnp.zeros((1, land), jnp.float32)
    for k in range(1, ny):
        turn_of = jnp.where(column == to_peer(k), 1.0 * k, turn_of)
    outer = (row < reach) | (row >= tr - reach)
    line = jnp.where(row < reach, row, row - (tr - EDGE))
    key = jnp.where(outer, (turn_of * chunks + chunk) * EDGE + line, -1.0)

    def one_hot(rows, key):
        line = lax.broadcasted_iota(jnp.int32, (rows, land), 0).astype(jnp.float32)
        return (line == key).astype(jnp.float32).T.astype(jnp.bfloat16)

    from_row[...] = one_hot(ny * chunks * EDGE, key)
    head, tail = chunk == 0.0, chunk == chunks - 1.0
    key = jnp.where((head | tail) & jnp.logical_not(outer), row, -1.0)
    for k in range(ny):
        from_col[:, k * tr : (k + 1) * tr] = one_hot(tr, jnp.where(turn_of == k, key, -1.0))
    line = lax.broadcasted_iota(jnp.int32, (LANES, land), 0)
    ends = ((line < reach) & head) | ((line >= LANES - reach) & tail)
    at_end[...] = ends.astype(jnp.float32).T

    for d in range(ny):
        place_t[d] = place[d].astype(jnp.float32).T.astype(jnp.bfloat16)

    settle_idx = take_idx.at[pl.ds(1, ny - 1)]
    if ny > 1:
        arrive(settle_idx, idx_r)
    line = lax.broadcasted_iota(jnp.int32, (land, cap), 0).astype(jnp.float32)
    for d in range(ny):
        target = (line == take_idx[d]).astype(jnp.float32)
        where_to[d] = target.astype(jnp.bfloat16)
        where_to_t[d] = target.T.astype(jnp.bfloat16)

    pltpu.make_async_copy(depth_in, h, in_sem.at[3]).wait()
    h[...] = h[...] * DEEP
    inflow = pick(where_to[0], give[0])
    for k in offsets(ny):
        if k == offsets(ny)[-1]:
            st_start()
        arrive(take.at[k], give_r.at[k - 1])
        inflow = inflow + pick(where_to[k], take[k])
    for c in range(chunks):
        at = (pl.ds(0, tr), pl.ds(c * LANES, LANES))
        h[at] = h[at] + DEEP * inflow[c * tr : (c + 1) * tr]

    h_rows[0] = h[0:EDGE, 0:tc]
    h_rows[1] = h[tr - EDGE : tr, 0:tc]
    h_cols[0], h_cols[1] = ends_of(h)
    h_start()
    keep(h, 4)

    for step in range(SUB):
        substep(step, h, bed, qe, qs, tile_face)

    high = lax.broadcasted_iota(jnp.int32, (tr, LANES), 0)
    within = (high >= reach) & (high < tr - reach)
    blocks = []
    for c in range(chunks):
        inside = within
        if c == 0:
            inside = inside & (lane >= reach)
        if c == chunks - 1:
            inside = inside & (lane < LANES - reach)
        blocks.append(jnp.where(inside, h[:, c * LANES : (c + 1) * LANES], 0.0))
    blocks = split(jnp.concatenate(blocks, axis=0))
    for k in offsets(ny)[::-1]:
        give_lev[k] = pick(where_to_t[k], blocks)
        send(give_lev.at[k], take_lev.at[k], data_s, lev_r.at[k - 1], from_peer(k))
    take_lev[0] = pick(where_to_t[0], blocks)

    gap = jnp.zeros((LANES // 2 - 2 * EDGE, tr), jnp.float32)
    half_gap = jnp.zeros((LANES // 2, tr), jnp.float32)
    lane8 = lane[:EDGE]

    def wrap(i, halo, west, east, corner_w, corner_e):
        side = jnp.concatenate([half_gap, east, gap, west], axis=0)
        rim[i, EDGE : 2 * EDGE] = halo
        flank[i, 0:tr] = jnp.where(own, flank[i, 0:tr], side.T)
        corner = jnp.where(lane8 < 3 * LANES // 4, corner_e, corner_w)
        far = pltpu.roll(halo[:, tc - LANES :], LANES // 2, 1)
        line = jnp.where(lane8 < LANES // 4, halo[:, :LANES], far)
        flank[i, tr : tr + EDGE] = jnp.where(low8, line, corner)

    def turn(x):
        return pltpu.roll(x, LANES // 2, 1)

    st_wait()
    nw, ne, sw, se = [st_in_corner[n] for n in range(4)]
    west_a, west_b = jnp.where(sub_low, sw, nw), half_turn(jnp.where(sub_low, nw, sw))
    east_a, east_b = jnp.where(sub_low, se, ne), half_turn(jnp.where(sub_low, ne, se))
    for i in range(2):
        up, down = st_in_rows[0, i], st_in_rows[1, i]
        west, east = st_in_cols[0, i], st_in_cols[1, i]
        cw = (west_a, west_b) if i == 0 else (turn(west_a), turn(west_b))
        ce = (turn(east_a), turn(east_b)) if i == 0 else (east_a, east_b)
        wrap(2 * i, jnp.where(sub_low, down, up), west, east, cw[0], ce[0])
        wrap(
            2 * i + 1, half_turn(jnp.where(sub_low, up, down)), half_turn(west),
            half_turn(east), cw[1], ce[1],
        )
    faces(rim[0], rim[1], rim_face)
    faces(flank[0], flank[1], flank_face)

    h_wait()
    nw, ne, sw, se = [h_in_corner[n] for n in range(4)]
    wrap(
        4, jnp.where(sub_low, h_in_rows[1], h_in_rows[0]), h_in_cols[0], h_in_cols[1],
        jnp.where(sub_low, sw, nw), turn(jnp.where(sub_low, se, ne)),
    )

    for step in range(SUB):
        for x, out in ((rim, rim_face), (flank, flank_face)):
            substep(step, x.at[4], x.at[0], x.at[2], x.at[3], out)

    def merge(i, x):
        x[0:EDGE] = jnp.where(sub_low, rim[i, 2 * EDGE : 3 * EDGE], x[0:EDGE])
        x[tr - EDGE : tr] = jnp.where(sub_low, x[tr - EDGE : tr], rim[i, 0:EDGE])
        edge = flank[i, 0:tr]
        x[:, 0:LANES] = jnp.where(lane < reach, edge, x[:, 0:LANES])
        x[:, tc - LANES : tc] = jnp.where(
            lane >= LANES - reach, turn(edge), x[:, tc - LANES : tc]
        )

    merge(4, h)
    give_edge[:, 0:tc] = jnp.where(sub_low, h[0:EDGE], h[tr - EDGE : tr])
    west, east = ends_of(h)
    give_edge[:, tc : tc + tr] = jnp.where(sub_low, west, east)
    for k in offsets(ny):
        send(give_edge, take_edge.at[k], data_s, edge_r, from_peer(k))
    take_edge[0] = give_edge[...]
    merge(2, qe)
    merge(3, qs)
    h[...] = h[...] * (1.0 / DEEP)
    qe[...] = qe[...] * (1.0 / FLOW)
    qs[...] = qs[...] * (1.0 / FLOW)
    store, rain = land_in[0], land_in[1]
    dry[...] = store + rain - rain * store * store
    gain[...] = INFIL_RATE * (1.0 - store)
    levels = pick(place_t[0], take_lev[0])
    for k in offsets(ny)[::-1]:
        arrive(take_lev.at[k], lev_r.at[k - 1])
        levels = levels + pick(place_t[k], take_lev[k])
    mine[...] = levels
    if ny > 1:
        arrive(take_edge.at[pl.ds(1, ny - 1)], edge_r)
    edge[...] = take_edge[...]
    if ny > 1:
        arrive(settle_idx, idx_s)
        settle(data_s, (ny - 1) * (2 * cap // EDGE + (tc + tr) // LANES))
    st_done()
    h_done()


def finish(
    h, qe, qs, dry, gain, mine, edge, from_row, from_col, at_end,
    depth_out, east_out, south_out, soil_out,
    newsoil, sem,
):
    ny, tr = edge.shape[0], h.shape[0]
    chunks = h.shape[1] // LANES
    copies = [
        pltpu.make_async_copy(src, dst, sem.at[i])
        for i, (src, dst) in enumerate(
            [(h, depth_out), (qe, east_out), (qs, south_out), (newsoil, soil_out)]
        )
    ]
    for c in copies[:-1]:
        c.start()
    table = [edge[k, :, c * LANES : (c + 1) * LANES] for k in range(ny) for c in range(chunks)]
    levels = mine[...] + pick(from_row[...], jnp.concatenate(table, axis=0))
    blank = jnp.zeros((LANES - 2 * EDGE, tr), jnp.float32)
    sides = []
    for k in range(ny):
        side = edge[k, :, chunks * LANES :]
        sides.append(jnp.concatenate([side, blank, side], axis=0).T)
    levels = levels + at_end[...] * pick(from_col[...], jnp.concatenate(sides, axis=0))
    newsoil[...] = dry[...] + gain[...] * (1.0 - jnp.exp(levels * (-1.0 / DEEP)))
    copies[-1].start()
    for c in copies:
        c.wait()


def local(depth, bed, east, south, rough, wet, soil, rain, column, block):
    nx, ny = lax.axis_size("gx"), lax.axis_size("gy")
    tr, tc = depth.shape
    land = soil.shape[1]
    cap = 2 * land // ny
    grid = (tr, tc)
    rim, flank = (3 * EDGE, tc), (tr + EDGE, LANES)
    f32, bf16, i32 = jnp.float32, jnp.bfloat16, jnp.int32
    v = pltpu.VMEM
    dma = pltpu.SemaphoreType.DMA
    peers = max(1, ny - 1)

    def edge_bufs(k):
        return [v((2, *k, EDGE, tc), f32), v((2, *k, EDGE, tr), f32)]

    corners = v((2, 2, EDGE, LANES), f32)
    in_corners = v((4, EDGE, LANES), f32)
    span = max(5 * tr * tc, peers * (2 * cap * LANES + EDGE * (tc + tr)), 4 * EDGE * (2 * tc + 2 * tr + 4 * LANES))
    any_ = pl.BlockSpec(memory_space=pltpu.MemorySpace.HBM)
    vmem = pl.BlockSpec(memory_space=pltpu.VMEM)
    shape = jax.ShapeDtypeStruct
    out = pl.pallas_call(
        functools.partial(kernel, nx, ny, cap),
        out_shape=[shape(grid, f32)] * 3
        + [shape((land, LANES), f32)] * 3
        + [shape((ny, EDGE, tc + tr), f32)]
        + [shape((land, ny * (tc // LANES) * EDGE), bf16), shape((land, ny * tr), bf16)]
        + [shape((land, LANES), f32)],
        in_specs=[any_] * 10,
        out_specs=[vmem] * 10,
        scratch_shapes=[v(grid, f32)] * 2
        + [v((tr, tc), i32)] * 2
        + [v((2, land, LANES), f32), v((2, 1, land), i32)]
        + [v((6, *grid), f32), v((5, *rim), f32), v((6, *rim), f32)]
        + [v((5, *flank), f32), v((6, *flank), f32)]
        + [v((ny, cap, LANES), f32)] * 2
        + [v((ny, 1, cap), f32)] * 2
        + [v((ny, cap, LANES), f32)] * 2
        + edge_bufs((2,)) + [corners] + edge_bufs((2,)) + [in_corners]
        + edge_bufs(()) + edge_bufs(()) + [in_corners]
        + [v((ny, cap, land), bf16), v((ny, land, cap), bf16)]
        + [v((ny, land, cap), bf16), v((ny, cap, land), bf16)]
        + [v((EDGE, tc + tr), f32), v((ny, EDGE, tc + tr), f32)]
        + [v((span // (EDGE * LANES), EDGE, LANES), f32)]
        + [dma((4,))]
        + [dma((peers,))] * 2
        + [dma] * 8,
        compiler_params=pltpu.CompilerParams(collective_id=0, has_side_effects=True, vmem_limit_bytes=24 << 20
        ),
    )(
        *(
            pltpu.with_memory_space_constraint(x, pltpu.MemorySpace.HBM)
            for x in (
                depth, bed, east, south, rough, wet, soil[0], rain[0],
                column.reshape(1, land), block,
            )
        )
    )
    out = pl.pallas_call(
        finish,
        out_shape=[shape((tr, tc), f32)] * 3 + [shape((land, LANES), f32)],
        in_specs=[vmem] * 10,
        out_specs=[any_] * 4,
        scratch_shapes=[v((land, LANES), f32), dma((4,))],
        compiler_params=pltpu.CompilerParams(vmem_limit_bytes=16 << 20),
    )(*out)
    return out[0], out[1], out[2], out[3][None]


def solution(mesh):
    grid = P("gx", "gy")
    blocks = P("gx", "gy", None)
    return jax.shard_map(
        local, mesh=mesh,
        in_specs=(grid,) * 6 + (blocks,) * 3 + (grid,),
        out_specs=(grid,) * 3 + (blocks,),
        check_vma=False,
    )
```

```python
import functools

import jax
import jax.numpy as jnp
from jax import lax
from jax.experimental import pallas as pl
from jax.experimental.pallas import tpu as pltpu
from jax.sharding import PartitionSpec as P

SUB = 4
GRAVITY = 9.81
TIME_STEP = 1.0
CELL_WIDTH = 30.0
DEPTH_FLOOR = 0.3
INFIL_RATE = 0.5
MANNING = (0.02, 0.03, 0.035, 0.045, 0.06, 0.08, 0.1, 0.15)
POWER = -7.0 / 3.0
STRIDE = TIME_STEP / CELL_WIDTH
DEEP = GRAVITY * STRIDE * STRIDE
FLOW = DEEP * STRIDE
DRAG = 0.5 * GRAVITY * TIME_STEP * DEEP ** (-POWER) / FLOW
LANES = 128
EDGE = 8
MESH = pl.DeviceIdType.MESH
AROUND = ((-1, -1), (-1, 0), (-1, 1), (0, -1), (0, 1), (1, -1), (1, 0), (1, 1))
NW, N, NE, W, E, SW, S, SE = range(8)


def split(x):
    a = x.astype(jnp.bfloat16)
    b = (x - a.astype(jnp.float32)).astype(jnp.bfloat16)
    return jnp.concatenate([a, b], axis=1)


def pick(mask, x):
    x = x if x.dtype == jnp.bfloat16 else split(x)
    y = jnp.dot(mask, x, preferred_element_type=jnp.float32)
    return y[:, :LANES] + y[:, LANES:]


def flip(i, k, n):
    if n & (n - 1):
        return None
    both, bit = 0, 1
    while bit < n:
        if k & bit:
            both = both + bit * lax.rem(i // bit, 2)
        bit *= 2
    return i + k - 2 * both


def offsets(n):
    return sorted(range(1, n), key=lambda k: bin(k).count("1"))


def east_of(x):
    return pltpu.roll(x, x.shape[1] - 1, 1)


def south_of(x):
    return pltpu.roll(x, x.shape[0] - 1, 0)


def face(eta, eta_next, base, coef, closed, q):
    depth = jnp.maximum(eta, eta_next) - base
    driving = jnp.maximum(depth, 0.0) * (eta_next - eta)
    power = jnp.exp2(jnp.log2(jnp.maximum(depth, DEEP * DEPTH_FLOOR)) * POWER)
    return (q - driving) / (closed + coef * jnp.abs(q) * power)


def kernel(
    nx, ny, cap,
    depth_in, bed_in, east_in, south_in, rough_in, wet_in, soil_in, rain_in, col_in, blk_in,
    h, qe, qs, dry, gain, mine, edge, from_row, from_col, at_end,
    bed, fric, rough, wet, land_in, index,
    tile_face, rim, rim_face, flank, flank_face,
    give, take, give_idx, take_idx, give_lev, take_lev,
    st_rows, st_cols, st_corner, st_in_rows, st_in_cols, st_in_corner,
    h_rows, h_cols, h_in_rows, h_in_cols, h_in_corner,
    place, place_t, where_to, where_to_t, before, give_edge, take_edge, span,
    in_sem, give_r, lev_r, edge_r, data_s, idx_s, idx_r, st_s, st_r, hs_s, hs_r,
):
    gx, gy = lax.axis_index("gx"), lax.axis_index("gy")
    tr, tc = rough.shape
    land = land_in.shape[1]
    chunks = tc // LANES

    loads = [
        pltpu.make_async_copy(src, dst, in_sem.at[i])
        for i, src, dst in [
            (0, col_in, index.at[0]), (0, blk_in, index.at[1]),
            (1, soil_in, land_in.at[0]), (1, rain_in, land_in.at[1]),
            (2, rough_in, rough), (2, wet_in, wet), (2, bed_in, bed),
            (2, east_in, qe), (2, south_in, qs), (3, depth_in, h),
        ]
    ]
    for c in loads:
        c.start()

    def settle(sem, tiles):
        ref = span.at[pl.ds(0, tiles)]
        pltpu.make_async_copy(ref, ref, sem).wait()

    def there(k):
        dx, dy = AROUND[k]
        x, y = gx + dx, gy + dy
        return (x >= 0) & (x < nx) & (y >= 0) & (y < ny)

    barrier = pltpu.get_barrier_semaphore()
    for k in range(1, ny):
        pl.semaphore_signal(
            barrier, inc=1, device_id=(gx, lax.rem(gy + k, ny)), device_id_type=MESH
        )
    total = ny - 1
    for k in (NW, N, NE, SW, S, SE):
        dx, dy = AROUND[k]

        @pl.when(there(k))
        def _(dx=dx, dy=dy):
            pl.semaphore_signal(barrier, inc=1, device_id=(gx + dx, gy + dy), device_id_type=MESH)

        total = total + there(k).astype(jnp.int32)

    for k, ref in ((N, (st_in_rows, h_in_rows)), (S, (st_in_rows, h_in_rows))):
        @pl.when(jnp.logical_not(there(k)))
        def _(k=k, ref=ref):
            for r in ref:
                r[int(k == S)] = jnp.zeros(r.shape[1:], r.dtype)
    for k, ref in ((W, (st_in_cols, h_in_cols)), (E, (st_in_cols, h_in_cols))):
        @pl.when(jnp.logical_not(there(k)))
        def _(k=k, ref=ref):
            for r in ref:
                r[int(k == E)] = jnp.zeros(r.shape[1:], r.dtype)
    for n, k in enumerate((NW, NE, SW, SE)):
        @pl.when(jnp.logical_not(there(k)))
        def _(n=n):
            for r in (st_in_corner, h_in_corner):
                r[n] = jnp.zeros(r.shape[1:], r.dtype)

    def to_peer(k):
        if k == 0:
            return gy
        peer = flip(gy, k, ny)
        return lax.rem(gy + k, ny) if peer is None else peer

    def from_peer(k):
        peer = flip(gy, k, ny)
        return lax.rem(gy + ny - k, ny) if peer is None else peer

    def send(src, dst, ss, rs, peer):
        pltpu.make_async_remote_copy(
            src_ref=src, dst_ref=dst, send_sem=ss, recv_sem=rs,
            device_id=(gx, peer), device_id_type=MESH,
        ).start()

    def arrive(dst, rs):
        pltpu.make_async_copy(dst, dst, rs).wait()

    ahead = lax.broadcasted_iota(jnp.int32, (land, land), 0) < lax.broadcasted_iota(
        jnp.int32, (land, land), 1
    )
    before[...] = ahead.astype(jnp.float32).astype(jnp.bfloat16)
    pltpu.make_async_copy(index, index, in_sem.at[0]).wait()
    column = index[0]
    groups = max(EDGE, ny)
    is_col = lax.broadcasted_iota(jnp.int32, (groups, land), 0) == column
    rank = jnp.dot(
        is_col.astype(jnp.float32).astype(jnp.bfloat16),
        before[...],
        preferred_element_type=jnp.float32,
    )
    rank = jnp.sum(jnp.where(is_col, rank, 0.0), axis=0, keepdims=True)
    slot = column.astype(jnp.float32) * cap + rank

    block = index[1].astype(jnp.float32)
    row = jnp.floor((block + 0.5) * (1.0 / chunks))
    chunk = block - row * chunks
    line = lax.broadcasted_iota(jnp.int32, (EDGE, land), 0)
    code = jnp.where(line == 0, row + 1.0, jnp.where(line == 1, chunk, 0.0))
    code = code.astype(jnp.bfloat16)
    seat = lax.broadcasted_iota(jnp.int32, (cap, land), 0).astype(jnp.float32)

    pltpu.make_async_copy(land_in, land_in, in_sem.at[1]).wait()
    runoff = split(land_in[1] * land_in[0] * land_in[0])

    def pack(k):
        hit = (seat == slot - (to_peer(k) * cap).astype(jnp.float32)).astype(jnp.float32)
        mask = hit.astype(jnp.bfloat16)
        place[k] = mask
        owner = lax.dot_general(
            code, mask, (((1,), (1,)), ((), ())), preferred_element_type=jnp.float32
        )
        give_idx[k] = owner[1:2] * tr + owner[0:1] - 1.0
        give[k] = pick(mask, runoff)

    for n, k in enumerate(offsets(ny)):
        pack(k)
        if n == 0:
            pl.semaphore_wait(barrier, total)
        send(give_idx.at[k], take_idx.at[k], idx_s, idx_r, to_peer(k))
        send(give.at[k], take.at[k], data_s, give_r.at[k - 1], to_peer(k))
    pack(0)
    take_idx[0] = give_idx[0]

    settle(in_sem.at[2], 5 * tr * tc // (EDGE * LANES))
    bed[...] = bed[...] * DEEP
    qe[...] = qe[...] * FLOW
    qs[...] = qs[...] * FLOW
    kind = rough[...]
    f = jnp.zeros((tr, tc), jnp.float32)
    for i, coefficient in enumerate(MANNING):
        f = jnp.where(kind == i, coefficient * coefficient, f)
    fric[...] = jnp.where(wet[...] > 0, f, -1.0)
    lane_low = lax.broadcasted_iota(jnp.int32, (tr, LANES), 1) < LANES // 2
    low8 = lane_low[:EDGE]
    sub_low = lax.broadcasted_iota(jnp.int32, (EDGE, 1), 0) < EDGE // 2
    half_turn = lambda x: pltpu.roll(x, EDGE // 2, 0)
    first, last = pl.ds(0, LANES), pl.ds(tc - LANES, LANES)

    def ends_of(ref):
        ends = jnp.where(lane_low, ref[0:tr, 0:LANES], ref[0:tr, tc - LANES : tc]).T
        return ends[0:EDGE], ends[LANES - EDGE :]

    pairs = ((bed, fric), (qe, qs))
    for i, (a, b) in enumerate(pairs):
        st_rows[0, i] = jnp.where(sub_low, a[0:EDGE, 0:tc], half_turn(b[0:EDGE, 0:tc]))
        st_rows[1, i] = jnp.where(
            sub_low, half_turn(b[tr - EDGE : tr, 0:tc]), a[tr - EDGE : tr, 0:tc]
        )
        (aw, ae), (bw, be) = ends_of(a), ends_of(b)
        st_cols[0, i] = jnp.where(sub_low, aw, half_turn(bw))
        st_cols[1, i] = jnp.where(sub_low, half_turn(be), ae)
    for dx in range(2):
        x, y = st_rows[dx, 0, :, first], st_rows[dx, 1, :, first]
        st_corner[dx, 0] = jnp.where(low8, x, pltpu.roll(y, LANES // 2, 1))
        x, y = st_rows[dx, 0, :, last], st_rows[dx, 1, :, last]
        st_corner[dx, 1] = jnp.where(low8, pltpu.roll(y, LANES // 2, 1), x)

    def edges(piece, tiles, ss, rs):
        def start():
            for k in (NW, NE, SW, SE, W, E, N, S):
                @pl.when(there(k))
                def _(k=k):
                    dx, dy = AROUND[k]
                    src, dst = piece(k)
                    pltpu.make_async_remote_copy(
                        src_ref=src, dst_ref=dst, send_sem=ss, recv_sem=rs,
                        device_id=(gx + dx, gy + dy), device_id_type=MESH,
                    ).start()

        def wait(sem):
            up = (gx > 0).astype(jnp.int32) + (gx < nx - 1).astype(jnp.int32)
            side = (gy > 0).astype(jnp.int32) + (gy < ny - 1).astype(jnp.int32)
            for r in range(3):
                for c in range(3):
                    n = r * tiles[0] + c * tiles[1] + r * c * tiles[2]
                    if n:
                        @pl.when((up == r) & (side == c))
                        def _(n=n):
                            settle(sem, n)

        return start, lambda: wait(rs), lambda: wait(ss)

    corner_at = {NW: 3, NE: 2, SW: 1, SE: 0}

    def st_piece(k):
        dx, dy = AROUND[k]
        if dy == 0:
            return st_rows.at[int(dx > 0)], st_in_rows.at[int(dx < 0)]
        if dx == 0:
            return st_cols.at[int(dy > 0)], st_in_cols.at[int(dy < 0)]
        return st_corner.at[int(dx > 0), int(dy > 0)], st_in_corner.at[corner_at[k]]

    def h_piece(k):
        dx, dy = AROUND[k]
        if dy == 0:
            return h_rows.at[int(dx > 0)], h_in_rows.at[int(dx < 0)]
        if dx == 0:
            return h_cols.at[int(dy > 0)], h_in_cols.at[int(dy < 0)]
        side = last if dy > 0 else first
        return h_rows.at[int(dx > 0), :, side], h_in_corner.at[corner_at[k]]

    st_start, st_wait, st_done = edges(
        st_piece, (2 * chunks, 2 * (tr // LANES), 1), st_s, st_r
    )
    h_start, h_wait, h_done = edges(h_piece, (chunks, tr // LANES, 1), hs_s, hs_r)

    lane = lax.broadcasted_iota(jnp.int32, (tr, LANES), 1)
    own = lane < LANES // 2

    def keep(x, i):
        rim[i, 0:EDGE] = x[tr - EDGE : tr, 0:tc]
        rim[i, 2 * EDGE : 3 * EDGE] = x[0:EDGE, 0:tc]
        flank[i, 0:tr] = jnp.where(
            lane < LANES // 4,
            x[0:tr, 0:LANES],
            pltpu.roll(x[0:tr, tc - LANES : tc], LANES // 2, 1),
        )

    def faces(b, fr, out):
        b_e, f_e, b_s, f_s = east_of(b), east_of(fr), south_of(b), south_of(fr)
        out[0] = jnp.maximum(b, b_e)
        out[1] = jnp.maximum(b, b_s)
        for i, other in ((2, f_e), (3, f_s)):
            is_open = (fr > 0.0) & (other > 0.0)
            out[i] = jnp.where(is_open, DRAG * (fr + other), 0.0)
            out[i + 2] = jnp.where(is_open, 1.0, jnp.inf)

    def substep(step, h, b, e, s, out):
        eta = h[...] + b[...] if step == 0 else h[...]
        east = face(eta, east_of(eta), out[0], out[2], out[4], e[...])
        south = face(eta, south_of(eta), out[1], out[3], out[5], s[...])
        e[...] = east
        s[...] = south
        eta = eta + (pltpu.roll(east, 1, 1) - east + pltpu.roll(south, 1, 0) - south)
        h[...] = eta - b[...] if step == SUB - 1 else eta

    for i, x in enumerate((bed, fric, qe, qs)):
        keep(x, i)
    faces(bed[...], fric[...], tile_face)

    reach = EDGE // 2
    turn_of = jnp.zeros((1, land), jnp.float32)
    for k in range(1, ny):
        turn_of = jnp.where(column == to_peer(k), 1.0 * k, turn_of)
    outer = (row < reach) | (row >= tr - reach)
    line = jnp.where(row < reach, row, row - (tr - EDGE))
    key = jnp.where(outer, (turn_of * chunks + chunk) * EDGE + line, -1.0)

    def one_hot(rows, key):
        line = lax.broadcasted_iota(jnp.int32, (rows, land), 0).astype(jnp.float32)
        return (line == key).astype(jnp.float32).T.astype(jnp.bfloat16)

    from_row[...] = one_hot(ny * chunks * EDGE, key)
    head, tail = chunk == 0.0, chunk == chunks - 1.0
    key = jnp.where((head | tail) & jnp.logical_not(outer), row, -1.0)
    for k in range(ny):
        from_col[:, k * tr : (k + 1) * tr] = one_hot(tr, jnp.where(turn_of == k, key, -1.0))
    line = lax.broadcasted_iota(jnp.int32, (LANES, land), 0)
    ends = ((line < reach) & head) | ((line >= LANES - reach) & tail)
    at_end[...] = ends.astype(jnp.float32).T

    for d in range(ny):
        place_t[d] = place[d].astype(jnp.float32).T.astype(jnp.bfloat16)

    settle_idx = take_idx.at[pl.ds(1, ny - 1)]
    if ny > 1:
        arrive(settle_idx, idx_r)
    line = lax.broadcasted_iota(jnp.int32, (land, cap), 0).astype(jnp.float32)
    for d in range(ny):
        target = (line == take_idx[d]).astype(jnp.float32)
        where_to[d] = target.astype(jnp.bfloat16)
        where_to_t[d] = target.T.astype(jnp.bfloat16)

    pltpu.make_async_copy(depth_in, h, in_sem.at[3]).wait()
    h[...] = h[...] * DEEP
    inflow = pick(where_to[0], give[0])
    for k in offsets(ny):
        if k == offsets(ny)[-1]:
            st_start()
        arrive(take.at[k], give_r.at[k - 1])
        inflow = inflow + pick(where_to[k], take[k])
    for c in range(chunks):
        at = (pl.ds(0, tr), pl.ds(c * LANES, LANES))
        h[at] = h[at] + DEEP * inflow[c * tr : (c + 1) * tr]

    h_rows[0] = h[0:EDGE, 0:tc]
    h_rows[1] = h[tr - EDGE : tr, 0:tc]
    h_cols[0], h_cols[1] = ends_of(h)
    h_start()
    keep(h, 4)

    for step in range(SUB):
        substep(step, h, bed, qe, qs, tile_face)

    high = lax.broadcasted_iota(jnp.int32, (tr, LANES), 0)
    within = (high >= reach) & (high < tr - reach)
    blocks = []
    for c in range(chunks):
        inside = within
        if c == 0:
            inside = inside & (lane >= reach)
        if c == chunks - 1:
            inside = inside & (lane < LANES - reach)
        blocks.append(jnp.where(inside, h[:, c * LANES : (c + 1) * LANES], 0.0))
    blocks = split(jnp.concatenate(blocks, axis=0))
    order = offsets(ny)[::-1]
    for group in (order[:1], order[1:]):
        for k in group:
            give_lev[k] = pick(where_to_t[k], blocks)
        for k in group:
            send(give_lev.at[k], take_lev.at[k], data_s, lev_r.at[k - 1], from_peer(k))

    gap = jnp.zeros((LANES // 2 - 2 * EDGE, tr), jnp.float32)
    half_gap = jnp.zeros((LANES // 2, tr), jnp.float32)
    lane8 = lane[:EDGE]

    def wrap(i, halo, west, east, corner_w, corner_e):
        side = jnp.concatenate([half_gap, east, gap, west], axis=0)
        rim[i, EDGE : 2 * EDGE] = halo
        flank[i, 0:tr] = jnp.where(own, flank[i, 0:tr], side.T)
        corner = jnp.where(lane8 < 3 * LANES // 4, corner_e, corner_w)
        far = pltpu.roll(halo[:, tc - LANES :], LANES // 2, 1)
        line = jnp.where(lane8 < LANES // 4, halo[:, :LANES], far)
        flank[i, tr : tr + EDGE] = jnp.where(low8, line, corner)

    def turn(x):
        return pltpu.roll(x, LANES // 2, 1)

    st_wait()
    nw, ne, sw, se = [st_in_corner[n] for n in range(4)]
    west_a, west_b = jnp.where(sub_low, sw, nw), half_turn(jnp.where(sub_low, nw, sw))
    east_a, east_b = jnp.where(sub_low, se, ne), half_turn(jnp.where(sub_low, ne, se))
    for i in range(2):
        up, down = st_in_rows[0, i], st_in_rows[1, i]
        west, east = st_in_cols[0, i], st_in_cols[1, i]
        cw = (west_a, west_b) if i == 0 else (turn(west_a), turn(west_b))
        ce = (turn(east_a), turn(east_b)) if i == 0 else (east_a, east_b)
        wrap(2 * i, jnp.where(sub_low, down, up), west, east, cw[0], ce[0])
        wrap(
            2 * i + 1, half_turn(jnp.where(sub_low, up, down)), half_turn(west),
            half_turn(east), cw[1], ce[1],
        )
    faces(rim[0], rim[1], rim_face)
    faces(flank[0], flank[1], flank_face)

    h_wait()
    nw, ne, sw, se = [h_in_corner[n] for n in range(4)]
    wrap(
        4, jnp.where(sub_low, h_in_rows[1], h_in_rows[0]), h_in_cols[0], h_in_cols[1],
        jnp.where(sub_low, sw, nw), turn(jnp.where(sub_low, se, ne)),
    )

    for step in range(SUB):
        for x, out in ((rim, rim_face), (flank, flank_face)):
            substep(step, x.at[4], x.at[0], x.at[2], x.at[3], out)

    def merge(i, x):
        x[0:EDGE] = jnp.where(sub_low, rim[i, 2 * EDGE : 3 * EDGE], x[0:EDGE])
        x[tr - EDGE : tr] = jnp.where(sub_low, x[tr - EDGE : tr], rim[i, 0:EDGE])
        edge = flank[i, 0:tr]
        x[:, 0:LANES] = jnp.where(lane < reach, edge, x[:, 0:LANES])
        x[:, tc - LANES : tc] = jnp.where(
            lane >= LANES - reach, turn(edge), x[:, tc - LANES : tc]
        )

    merge(4, h)
    give_edge[:, 0:tc] = jnp.where(sub_low, h[0:EDGE], h[tr - EDGE : tr])
    west, east = ends_of(h)
    give_edge[:, tc : tc + tr] = jnp.where(sub_low, west, east)
    for k in offsets(ny)[::-1]:
        send(give_edge, take_edge.at[k], data_s, edge_r, from_peer(k))
    take_edge[0] = give_edge[...]
    take_lev[0] = pick(where_to_t[0], blocks)
    merge(2, qe)
    merge(3, qs)
    h[...] = h[...] * (1.0 / DEEP)
    qe[...] = qe[...] * (1.0 / FLOW)
    qs[...] = qs[...] * (1.0 / FLOW)
    store, rain = land_in[0], land_in[1]
    dry[...] = store + rain - rain * store * store
    gain[...] = INFIL_RATE * (1.0 - store)
    levels = pick(place_t[0], take_lev[0])
    for k in offsets(ny)[::-1]:
        arrive(take_lev.at[k], lev_r.at[k - 1])
        levels = levels + pick(place_t[k], take_lev[k])
    mine[...] = levels
    if ny > 1:
        arrive(take_edge.at[pl.ds(1, ny - 1)], edge_r)
    edge[...] = take_edge[...]
    if ny > 1:
        arrive(settle_idx, idx_s)
        settle(data_s, (ny - 1) * (2 * cap // EDGE + (tc + tr) // LANES))
    st_done()
    h_done()


def finish(
    h, qe, qs, dry, gain, mine, edge, from_row, from_col, at_end,
    depth_out, east_out, south_out, soil_out,
    newsoil, sem,
):
    ny, tr = edge.shape[0], h.shape[0]
    chunks = h.shape[1] // LANES
    copies = [
        pltpu.make_async_copy(src, dst, sem.at[i])
        for i, (src, dst) in enumerate(
            [(h, depth_out), (qe, east_out), (qs, south_out), (newsoil, soil_out)]
        )
    ]
    for c in copies[:-1]:
        c.start()
    table = [edge[k, :, c * LANES : (c + 1) * LANES] for k in range(ny) for c in range(chunks)]
    table = split(jnp.concatenate(table, axis=0))
    blank = jnp.zeros((LANES - 2 * EDGE, tr), jnp.float32)
    sides = []
    for k in range(ny):
        side = edge[k, :, chunks * LANES :]
        sides.append(jnp.concatenate([side, blank, side], axis=0).T)
    sides = split(jnp.concatenate(sides, axis=0))
    half = mine.shape[0] // 2
    for i in range(2):
        at = pl.ds(i * half, half)
        levels = mine[at] + pick(from_row[at], table)
        levels = levels + at_end[at] * pick(from_col[at], sides)
        newsoil[at] = dry[at] + gain[at] * (1.0 - jnp.exp(levels * (-1.0 / DEEP)))
        pltpu.make_async_copy(newsoil.at[at], soil_out.at[at], sem.at[3]).start()
    for c in copies:
        c.wait()


def local(depth, bed, east, south, rough, wet, soil, rain, column, block):
    nx, ny = lax.axis_size("gx"), lax.axis_size("gy")
    tr, tc = depth.shape
    land = soil.shape[1]
    cap = 2 * land // ny
    grid = (tr, tc)
    rim, flank = (3 * EDGE, tc), (tr + EDGE, LANES)
    f32, bf16, i32 = jnp.float32, jnp.bfloat16, jnp.int32
    v = pltpu.VMEM
    dma = pltpu.SemaphoreType.DMA
    peers = max(1, ny - 1)

    def edge_bufs(k):
        return [v((2, *k, EDGE, tc), f32), v((2, *k, EDGE, tr), f32)]

    corners = v((2, 2, EDGE, LANES), f32)
    in_corners = v((4, EDGE, LANES), f32)
    span = max(5 * tr * tc, peers * (2 * cap * LANES + EDGE * (tc + tr)), 4 * EDGE * (2 * tc + 2 * tr + 4 * LANES))
    any_ = pl.BlockSpec(memory_space=pltpu.MemorySpace.HBM)
    vmem = pl.BlockSpec(memory_space=pltpu.VMEM)
    shape = jax.ShapeDtypeStruct
    out = pl.pallas_call(
        functools.partial(kernel, nx, ny, cap),
        out_shape=[shape(grid, f32)] * 3
        + [shape((land, LANES), f32)] * 3
        + [shape((ny, EDGE, tc + tr), f32)]
        + [shape((land, ny * (tc // LANES) * EDGE), bf16), shape((land, ny * tr), bf16)]
        + [shape((land, LANES), f32)],
        in_specs=[any_] * 10,
        out_specs=[vmem] * 10,
        scratch_shapes=[v(grid, f32)] * 2
        + [v((tr, tc), i32)] * 2
        + [v((2, land, LANES), f32), v((2, 1, land), i32)]
        + [v((6, *grid), f32), v((5, *rim), f32), v((6, *rim), f32)]
        + [v((5, *flank), f32), v((6, *flank), f32)]
        + [v((ny, cap, LANES), f32)] * 2
        + [v((ny, 1, cap), f32)] * 2
        + [v((ny, cap, LANES), f32)] * 2
        + edge_bufs((2,)) + [corners] + edge_bufs((2,)) + [in_corners]
        + edge_bufs(()) + edge_bufs(()) + [in_corners]
        + [v((ny, cap, land), bf16), v((ny, land, cap), bf16)]
        + [v((ny, land, cap), bf16), v((ny, cap, land), bf16)]
        + [v((land, land), bf16), v((EDGE, tc + tr), f32), v((ny, EDGE, tc + tr), f32)]
        + [v((span // (EDGE * LANES), EDGE, LANES), f32)]
        + [dma((4,))]
        + [dma((peers,))] * 2
        + [dma] * 8,
        compiler_params=pltpu.CompilerParams(collective_id=0, has_side_effects=True, vmem_limit_bytes=24 << 20
        ),
    )(
        *(
            pltpu.with_memory_space_constraint(x, pltpu.MemorySpace.HBM)
            for x in (
                depth, bed, east, south, rough, wet, soil[0], rain[0],
                column.reshape(1, land), block,
            )
        )
    )
    out = pl.pallas_call(
        finish,
        out_shape=[shape((tr, tc), f32)] * 3 + [shape((land, LANES), f32)],
        in_specs=[vmem] * 10,
        out_specs=[any_] * 4,
        scratch_shapes=[v((land, LANES), f32), dma((4,))],
        compiler_params=pltpu.CompilerParams(vmem_limit_bytes=16 << 20),
    )(*out)
    return out[0], out[1], out[2], out[3][None]


def solution(mesh):
    grid = P("gx", "gy")
    blocks = P("gx", "gy", None)
    return jax.shard_map(
        local, mesh=mesh,
        in_specs=(grid,) * 6 + (blocks,) * 3 + (grid,),
        out_specs=(grid,) * 3 + (blocks,),
        check_vma=False,
    )
```
